32 devices in a mesh: mode: 4 (over z), ra: 2 (over y), rb: 4 (over x, core).
Axes of the slice: x: 2, y: 2, z: 4, core: 2. Of those that a mesh axis runs over, the one named last changes fastest.
Arguments:
- density_slab: float32 [1024, 32, 512], P('mode', 'ra', 'rb'), may hold values from -111 to 111
- start_basis: float32 [1024, 256], replicated, may hold values from -4 to 4
Outputs:
- projected_slab: float32 [256, 32, 512], P('mode', 'ra', 'rb')
The draws below stay inside these ranges and needn't reach their ends.
All inputs are finite; a program needn't handle non-finite values.
Results may differ from the reference program's by a relative error of at most 0.0002.
Values sent between devices are 32-bit elements; how exact they have to be, the bound alone decides.
No kernel may reach another device: no remote copies, remote signals or barrier semaphores. Data moves between devices by JAX's collectives and lax.ppermute only.
A program may use at most 64 MiB of HBM per device.

```python
import math
import jax
import jax.numpy as jnp
from jax import lax

WIDTH = 1024
RANK = 256
ITERS = 2
NJ = 32
NK = 512


def draw_density_slab(key, part):
    key_noise, key_scale, key_rough = jax.random.split(key, 3)
    noise = jnp.clip(jax.random.normal(key_noise, (WIDTH, NJ, NK), jnp.float32), -5.0, 5.0)
    mixed = noise + 0.45 * jnp.roll(noise, 1, axis=0) - 0.3 * jnp.roll(noise, 3, axis=0)
    scales = jnp.exp(jax.random.uniform(key_scale, (WIDTH, 1, 1), jnp.float32, 0.0, math.log(3.0)))
    rising = 1.0 + 2.0 * jnp.arange(NJ, dtype=jnp.float32).reshape(1, NJ, 1) / max(NJ - 1, 1)
    rough = jax.random.uniform(key_rough, (1, NJ, NK), jnp.float32, 0.6, 1.4)
    return scales * rising * rough * mixed


def draw_start_basis(key, part):
    key_values = jax.random.fold_in(key, 7)
    return jnp.clip(jax.random.normal(key_values, (WIDTH, RANK), jnp.float32), -4.0, 4.0)


def setup_inputs(seed: int = 0) -> dict:
    key_list = jax.random.split(jax.random.key(seed), 3)
    return {
        "density_slab": draw_density_slab(jax.random.fold_in(key_list[2], 71), 0),
        "start_basis": draw_start_basis(jax.random.fold_in(key_list[2], 71), 0),
    }


highest = lax.Precision.HIGHEST

def orthonormalize(matrix):
    inner = jnp.dot(matrix.T.astype(jnp.float32), matrix.astype(jnp.float32), precision=highest, preferred_element_type=jnp.float32)
    factor = jnp.linalg.cholesky(inner)
    return lax.linalg.triangular_solve(factor, matrix, left_side=False, lower=True, transpose_a=True)

def reference(density_slab, start_basis):
    fibre_rows = density_slab.reshape(WIDTH, NJ * NK)
    gram_total = jnp.dot(fibre_rows.astype(jnp.float32), fibre_rows.T.astype(jnp.float32), precision=highest, preferred_element_type=jnp.float32)
    basis_now = start_basis
    for repeat_index in range(ITERS):
        basis_now = orthonormalize(jnp.dot(gram_total.astype(jnp.float32), basis_now.astype(jnp.float32), precision=highest, preferred_element_type=jnp.float32))
    projected = jnp.dot(basis_now.T.astype(jnp.float32), fibre_rows.astype(jnp.float32), precision=highest, preferred_element_type=jnp.float32)
    return projected.reshape(RANK, NJ, NK)
```

```python
import jax
import jax.numpy as jnp
from jax import lax
from jax.sharding import PartitionSpec as P

ITERS = 2

highest = lax.Precision.HIGHEST


def orthonormalize(matrix):
    inner = jnp.dot(matrix.T, matrix, precision=highest, preferred_element_type=jnp.float32)
    factor = jnp.linalg.cholesky(inner)
    return lax.linalg.triangular_solve(
        factor, matrix, left_side=False, lower=True, transpose_a=True
    )


def exchange(block, axis, bit):
    size = lax.axis_size(axis)
    return lax.ppermute(block, axis, [(k, k ^ bit) for k in range(size)])


def bits_of(axis):
    return [1 << b for b in range(lax.axis_size(axis).bit_length() - 1)]


def all_reduce(partial):
    stages = [(axis, bit) for axis in ("rb", "ra") for bit in bits_of(axis)]
    width = partial.shape[1]
    held = partial
    for axis, bit in stages:
        side = (lax.axis_index(axis) // bit) % 2
        halves = held.reshape(2, -1, width)
        keep = lax.dynamic_index_in_dim(halves, side, 0, keepdims=False)
        send = lax.dynamic_index_in_dim(halves, 1 - side, 0, keepdims=False)
        held = keep + exchange(send, axis, bit)
    for bit in bits_of("mode"):
        held = held + exchange(held, "mode", bit)
    for axis, bit in stages[::-1]:
        side = (lax.axis_index(axis) // bit) % 2
        got = exchange(held, axis, bit)
        held = jnp.where(
            side == 0, jnp.concatenate([held, got]), jnp.concatenate([got, held])
        )
    return held


def turned(blocks, count, here):
    return jnp.concatenate(
        [
            lax.dynamic_index_in_dim(blocks, (here - d) % count, 0, keepdims=True)
            for d in range(count)
        ]
    )


def body(density_slab, start_basis):
    count = lax.axis_size("mode")
    here = lax.axis_index("mode")
    rows, nj, nk = density_slab.shape
    rank = start_basis.shape[1]
    pieces = density_slab.transpose(1, 0, 2).reshape(count, nj // count, rows, nk)
    arrived = []
    for d in range(count):
        piece = lax.dynamic_index_in_dim(pieces, (here + d) % count, 0, keepdims=False)
        if d:
            piece = lax.ppermute(piece, "mode", [(k, (k + d) % count) for k in range(count)])
        arrived.append(piece)
    fibres = jnp.concatenate(arrived, axis=1)

    def to_turned(matrix):
        return turned(matrix.reshape(count, rows, rank), count, here).reshape(-1, rank)

    def gram_apply(matrix_turned):
        inner = jnp.einsum("jik,ir->jkr", fibres, matrix_turned, precision=highest)
        return jnp.einsum("jik,jkr->ir", fibres, inner, precision=highest)

    basis_now = start_basis
    for repeat_index in range(ITERS):
        applied = to_turned(gram_apply(to_turned(basis_now)))
        basis_now = orthonormalize(all_reduce(applied))
    projected = jnp.einsum(
        "ir,jik->rjk", to_turned(basis_now), fibres, precision=highest
    )
    blocks = projected.reshape(count, rank // count, nj // count, nk)
    back = []
    for d in range(count):
        piece = lax.dynamic_index_in_dim(blocks, (here + d) % count, 0, keepdims=False)
        if d:
            piece = lax.ppermute(piece, "mode", [(k, (k + d) % count) for k in range(count)])
        back.append(piece)
    out = turned(jnp.stack(back), count, here)
    return out.transpose(1, 0, 2, 3).reshape(rank // count, nj, nk)


def solution(mesh):
    in_specs = (P("mode", "ra", "rb"), P())
    out_specs = P("mode", "ra", "rb")
    return jax.shard_map(body, mesh=mesh, in_specs=in_specs, out_specs=out_specs, check_vma=False)
```

```python
import functools

import jax
import jax.numpy as jnp
from jax import lax
from jax.experimental import pallas as pl
from jax.experimental.pallas import tpu as pltpu
from jax.sharding import PartitionSpec as P

SUB, LANES = 8, 128
HALF = LANES // 2
VMEM_BYTES = 56 * 2**20
LIFT = 2.0**20


def mm(a, b, a_dim, b_dim):
    return lax.dot_general(
        a,
        b,
        (((a_dim,), (b_dim,)), ((), ())),
        precision=lax.Precision.HIGHEST,
        preferred_element_type=jnp.float32,
    )


def eliminate(groups):
    sub = lax.broadcasted_iota(jnp.int32, (SUB, LANES), 0)
    done = []
    for p in range(len(groups)):
        first = p * SUB
        rows = [jnp.broadcast_to(groups[p][j : j + 1, :], (SUB, LANES)) for j in range(SUB)]
        block = [
            [
                jnp.broadcast_to(rows[i][:, first + j : first + j + 1], (SUB, LANES)) if j >= i else None
                for j in range(SUB)
            ]
            for i in range(SUB)
        ]
        lower = [[None] * SUB for _ in range(SUB)]
        inverse = []
        for i in range(SUB):
            inverse.append(1.0 / block[i][i])
            for j in range(i + 1, SUB):
                lower[j][i] = block[i][j] * inverse[i]
            for j in range(i + 1, SUB):
                for m in range(j, SUB):
                    block[j][m] = block[j][m] - lower[j][i] * block[i][m]
            for j in range(i + 1, SUB):
                rows[j] = rows[j] - lower[j][i] * rows[i]
        scaled = [rows[i] * inverse[i] for i in range(SUB)]
        for g in range(p + 1, len(groups)):
            tile = groups[g]
            columns = [
                jnp.broadcast_to(tile[:, first + j : first + j + 1], (SUB, LANES)) for j in range(SUB)
            ]
            for i in range(SUB):
                for j in range(i + 1, SUB):
                    columns[j] = columns[j] - columns[i] * lower[j][i]
            for i in range(SUB):
                tile = tile - columns[i] * scaled[i]
            groups[g] = tile
        out = rows[0] * lax.rsqrt(block[0][0])
        for i in range(1, SUB):
            out = jnp.where(sub == i, rows[i] * lax.rsqrt(block[i][i]), out)
        done.append(out)
    return done


def inverse_factor(inner, work):
    order = inner.shape[0]
    lane = lax.broadcasted_iota(jnp.int32, (SUB, LANES), 1)
    sub = lax.broadcasted_iota(jnp.int32, (SUB, LANES), 0)
    row = lax.broadcasted_iota(jnp.int32, (order, order), 0)
    col = lax.broadcasted_iota(jnp.int32, (order, order), 1)
    work[:, :order] = inner
    work[:, order:] = (row == col).astype(jnp.float32)
    for top in range(0, order, HALF):
        low = top + HALF
        groups = []
        for g in range(HALF // SUB):
            tile = work[top + g * SUB : top + (g + 1) * SUB, top:low]
            unit = (lane == sub + (g * SUB + HALF)).astype(jnp.float32)
            groups.append(jnp.concatenate([tile, unit[:, HALF:]], axis=1))
        small = jnp.concatenate([tile[:, HALF:] for tile in eliminate(groups)], axis=0)
        wide = mm(small, work[top:low, :], 1, 0)
        if low < order:
            work[low:, :] = work[low:, :] - mm(wide[:, low:order], wide, 0, 0)
        work[top:low, :] = wide
    return work[:, order:]


def flat(block_ref):
    return jnp.concatenate([block_ref[j] for j in range(block_ref.shape[0])], axis=1)


def place(d, count, rows):
    here = lax.axis_index("mode")
    return pl.ds(pl.multiple_of(lax.rem(here - d + count, count) * rows, LANES if rows % LANES == 0 else rows), rows)


def first_kernel(basis_ref, *refs):
    *blocks, out_ref = refs
    count, rows = len(blocks), blocks[0].shape[1]
    inner = None
    for d, block in enumerate(blocks):
        term = mm(basis_ref[place(d, count, rows), :], flat(block), 0, 0)
        inner = term if inner is None else inner + term
    for d, block in enumerate(blocks):
        out_ref[d] = mm(inner, flat(block), 1, 1)


def second_kernel(turned_ref, *refs):
    *blocks, out_ref = refs
    inner = None
    for d, block in enumerate(blocks):
        term = mm(turned_ref[d], flat(block), 1, 0)
        inner = term if inner is None else inner + term
    inner = inner * LIFT
    for d, block in enumerate(blocks):
        out_ref[d] = mm(inner, flat(block), 1, 1)


def factor_kernel(matrix_ref, out_ref, work):
    matrix = matrix_ref[...]
    out_ref[...] = inverse_factor(mm(matrix, matrix, 1, 1), work) * (1.0 / LIFT)


def last_kernel(turned_ref, factor_ref, *refs):
    *blocks, out_ref, work, held = refs
    count, width = len(blocks), blocks[0].shape[0]
    factor = factor_ref[...]
    inner = None
    projected = None
    for d, block in enumerate(blocks):
        basis = mm(factor, turned_ref[d], 1, 0)
        term = mm(basis, basis, 1, 1)
        inner = term if inner is None else inner + term
        term = mm(basis, flat(block), 1, 0)
        projected = term if projected is None else projected + term
    held[...] = projected
    projected = mm(inverse_factor(inner, work), held[...], 1, 0)
    for j in range(width):
        out_ref[j] = projected[:, j * LANES : (j + 1) * LANES]


def call(kernel, out_shape, scratch, *operands):
    whole = pl.BlockSpec(memory_space=pltpu.VMEM)
    return pl.pallas_call(
        kernel,
        out_shape=jax.ShapeDtypeStruct(out_shape, jnp.float32),
        in_specs=[whole] * len(operands),
        out_specs=whole,
        scratch_shapes=[pltpu.VMEM(shape, jnp.float32) for shape in scratch],
        compiler_params=pltpu.CompilerParams(vmem_limit_bytes=VMEM_BYTES),
    )(*operands)


def exchange(block, axis, bit):
    size = lax.axis_size(axis)
    return lax.ppermute(block, axis, [(k, k ^ bit) for k in range(size)])


def bits_of(axis):
    return [1 << b for b in range(lax.axis_size(axis).bit_length() - 1)]


def all_reduce(partial):
    stages = [(axis, bit) for axis in ("rb", "ra") for bit in bits_of(axis)]
    width = partial.shape[1]
    held = partial
    for axis, bit in stages:
        side = (lax.axis_index(axis) // bit) % 2
        halves = held.reshape(2, -1, width)
        keep = lax.dynamic_index_in_dim(halves, side, 0, keepdims=False)
        send = lax.dynamic_index_in_dim(halves, 1 - side, 0, keepdims=False)
        held = keep + exchange(send, axis, bit)
    for bit in bits_of("mode"):
        held = held + exchange(held, "mode", bit)
    for axis, bit in stages[::-1]:
        side = (lax.axis_index(axis) // bit) % 2
        got = exchange(held, axis, bit)
        held = jnp.where(
            side == 0, jnp.concatenate([held, got]), jnp.concatenate([got, held])
        )
    return held


def turned(blocks, count, here):
    return jnp.stack(
        [
            lax.dynamic_index_in_dim(blocks, (here - d) % count, 0, keepdims=False)
            for d in range(count)
        ]
    )


def shifts(blocks, count, here):
    arrived = []
    for d in range(count):
        piece = lax.dynamic_index_in_dim(blocks, (here + d) % count, 0, keepdims=False)
        if d:
            piece = lax.ppermute(piece, "mode", [(k, (k + d) % count) for k in range(count)])
        arrived.append(piece)
    return arrived


def body(density_slab, start_basis):
    count = lax.axis_size("mode")
    here = lax.axis_index("mode")
    rows, nj, nk = density_slab.shape
    width, rank = start_basis.shape
    pieces = density_slab.transpose(1, 0, 2).reshape(count, nj // count, rows, nk)
    blocks = shifts(pieces, count, here)

    def whole(arrived):
        return turned(arrived, count, here).transpose(1, 0, 2).reshape(rank, width)

    def split(matrix):
        return turned(matrix.reshape(rank, count, rows).transpose(1, 0, 2), count, here)

    shape = (count, rank, rows)
    work = (rank, 2 * rank)
    applied = all_reduce(whole(call(first_kernel, shape, [], start_basis, *blocks)))
    again = all_reduce(whole(call(second_kernel, shape, [], split(applied), *blocks)))
    factor = call(factor_kernel, (rank, rank), [work], applied)
    projected = call(
        last_kernel,
        (nj // count, rank, nk),
        [work, (rank, nj // count * nk)],
        split(again),
        factor,
        *blocks,
    )
    outward = projected.reshape(nj // count, count, rank // count, nk).transpose(1, 0, 2, 3)
    out = turned(jnp.stack(shifts(outward, count, here)), count, here)
    return out.reshape(nj, rank // count, nk).transpose(1, 0, 2)


def solution(mesh):
    in_specs = (P("mode", "ra", "rb"), P())
    out_specs = P("mode", "ra", "rb")
    return jax.shard_map(body, mesh=mesh, in_specs=in_specs, out_specs=out_specs, check_vma=False)
```

```python
import functools

import jax
import jax.numpy as jnp
from jax import lax
from jax.experimental import pallas as pl
from jax.experimental.pallas import tpu as pltpu
from jax.sharding import PartitionSpec as P


SUB, LANES = 8, 128
HALF = LANES // 2
VMEM_BYTES = 20 * 2**20
LIFT = 2.0**20


def mm(a, b, a_dim, b_dim):
    return lax.dot_general(
        a,
        b,
        (((a_dim,), (b_dim,)), ((), ())),
        precision=lax.Precision.HIGHEST,
        preferred_element_type=jnp.float32,
    )


def eliminate(groups, ones):
    sub = lax.broadcasted_iota(jnp.int32, (SUB, LANES), 0)
    done = []
    for p in range(len(groups)):
        first = p * SUB
        rows = [jnp.broadcast_to(groups[p][j : j + 1, :], (SUB, LANES)) for j in range(SUB)]
        across = [
            jnp.broadcast_to(groups[p][:, first + j : first + j + 1], (SUB, LANES)) * ones for j in range(SUB)
        ]
        block = [
            [jnp.broadcast_to(across[j][i : i + 1, :], (SUB, LANES)) if j >= i else None for j in range(SUB)]
            for i in range(SUB)
        ]
        lower = [[None] * SUB for _ in range(SUB)]
        inverse = []
        for i in range(SUB):
            inverse.append(1.0 / block[i][i])
            for j in range(i + 1, SUB):
                lower[j][i] = block[i][j] * inverse[i]
            for j in range(i + 1, SUB):
                for m in range(j, SUB):
                    block[j][m] = block[j][m] - lower[j][i] * block[i][m]
            for j in range(i + 1, SUB):
                rows[j] = rows[j] - lower[j][i] * rows[i]
        scaled = [rows[i] * inverse[i] for i in range(SUB)]
        for g in range(p + 1, len(groups)):
            tile = groups[g]
            columns = [
                jnp.broadcast_to(tile[:, first + j : first + j + 1], (SUB, LANES)) for j in range(SUB)
            ]
            for i in range(SUB):
                for j in range(i + 1, SUB):
                    columns[j] = columns[j] - columns[i] * lower[j][i]
            for i in range(SUB):
                tile = tile - columns[i] * scaled[i]
            groups[g] = tile
        out = rows[0] * lax.rsqrt(block[0][0])
        for i in range(1, SUB):
            out = jnp.where(sub == i, rows[i] * lax.rsqrt(block[i][i]), out)
        done.append(out)
    return done


def begin(inner, work):
    order = inner.shape[0]
    row = lax.broadcasted_iota(jnp.int32, (order, order), 0)
    col = lax.broadcasted_iota(jnp.int32, (order, order), 1)
    work[:, :order] = inner
    work[:, order:] = (row == col).astype(jnp.float32)


def step(work, top, ones):
    order = work.shape[0]
    low = top + HALF
    lane = lax.broadcasted_iota(jnp.int32, (SUB, LANES), 1)
    sub = lax.broadcasted_iota(jnp.int32, (SUB, LANES), 0)
    groups = []
    for g in range(HALF // SUB):
        tile = work[top + g * SUB : top + (g + 1) * SUB, top:low]
        unit = (lane == sub + (g * SUB + HALF)).astype(jnp.float32)
        groups.append(jnp.concatenate([tile, unit[:, HALF:]], axis=1))
    small = jnp.concatenate([tile[:, HALF:] for tile in eliminate(groups, ones)], axis=0)
    wide = mm(small, work[top:low, :], 1, 0)
    if low < order:
        work[low:, :] = work[low:, :] - mm(wide[:, low:order], wide, 0, 0)
    work[top:low, :] = wide


def lanes(d, count, rows):
    if rows % LANES:
        return pl.ds(d * rows, rows)
    here = lax.axis_index("mode")
    return pl.ds(pl.multiple_of(lax.rem(here - d + count, count) * rows, rows), rows)


def stage_side(stage):
    axis, bit = stage
    return lax.rem(lax.axis_index(axis) // bit, 2)


def row_places(stages, height):
    members = 1 << (len(stages) - 1)
    share = height // (2 * members)
    mine = sum((stage_side(stage) << index) for index, stage in enumerate(stages[1:]))
    side = stage_side(stages[0])
    return [
        [pl.ds(pl.multiple_of((top * members + (mine ^ d)) * share, share), share) for d in range(members)]
        for top in (side, 1 - side)
    ]


def gather_rows(parts, stages, matrix):
    for part, places in zip(parts, row_places(stages, matrix.shape[0])):
        share = part.shape[0] // len(places)
        for d, place in enumerate(places):
            matrix[place, :] = part[d * share : (d + 1) * share, :]


def spread_out(inner, blocks, outs, stages, matrix):
    count, rows = len(blocks), blocks[0].shape[0]
    for d, block in enumerate(blocks):
        matrix[:, lanes(d, count, rows)] = mm(inner, block[...], 1, 1)
    for out, places in zip(outs, row_places(stages, matrix.shape[0])):
        share = out.shape[0] // len(places)
        for d, place in enumerate(places):
            out[d * share : (d + 1) * share, :] = matrix[place, :]


def first_kernel(count, stages, basis_ref, *refs):
    blocks, outs, matrix = refs[:count], refs[count:-1], refs[-1]
    rows = blocks[0].shape[0]
    here = lax.axis_index("mode")
    inner = None
    for d, block in enumerate(blocks):
        place = pl.ds(pl.multiple_of(lax.rem(here - d + count, count) * rows, rows), rows)
        term = mm(basis_ref[place, :], block[...], 0, 0)
        inner = term if inner is None else inner + term
    spread_out(inner, blocks, outs, stages, matrix)


def second_kernel(count, inputs, stages, *refs):
    parts, blocks = refs[:inputs], refs[inputs : inputs + count]
    outs, matrix = refs[inputs + count : -1], refs[-1]
    rows = blocks[0].shape[0]
    gather_rows(parts, stages, matrix)
    inner = None
    for d, block in enumerate(blocks):
        term = mm(matrix[:, lanes(d, count, rows)], block[...], 1, 0)
        inner = term if inner is None else inner + term
    spread_out(inner * LIFT, blocks, outs, stages, matrix)


def inner_kernel(stages, *refs):
    *parts, work, matrix = refs
    gather_rows(parts, stages, matrix)
    whole = matrix[...]
    begin(mm(whole, whole, 1, 1), work)


def step_kernel(top, work_ref, work, ones):
    ones[...] = jnp.ones_like(ones)
    work[...] = work_ref[...]
    step(work, top, ones[...])


def last_kernel(count, inputs, stages, work_ref, *refs):
    parts, blocks = refs[:inputs], refs[inputs : inputs + count]
    outs, (work, matrix, held, ones) = refs[inputs + count : -4], refs[-4:]
    rank, rows = matrix.shape[0], blocks[0].shape[0]
    gather_rows(parts, stages, matrix)
    factor = work_ref[:, rank:] * (1.0 / LIFT)
    inner = None
    projected = None
    for d, block in enumerate(blocks):
        basis = mm(factor, matrix[:, lanes(d, count, rows)], 1, 0)
        term = mm(basis, basis, 1, 1)
        inner = term if inner is None else inner + term
        term = mm(basis, block[...], 1, 0)
        projected = term if projected is None else projected + term
    held[...] = projected
    begin(inner, work)
    ones[...] = jnp.ones_like(ones)
    for top in range(0, rank, HALF):
        step(work, top, ones[...])
    held[...] = mm(work[:, rank:], held[...], 1, 0)
    here = lax.axis_index("mode")
    part = rank // count
    for d, out in enumerate(outs):
        place = pl.ds(pl.multiple_of(lax.rem(here + d, count) * part, part), part)
        out[...] = held[place, :]


def pick_kernel(distances, count, fibres, slab_ref, *outs):
    rows, width = outs[0].shape
    share = width // LANES
    for d, out in zip(distances, outs):
        target = lax.rem(lax.axis_index("mode") + d, count)
        for j in range(share):
            start = target * share + j
            out[:, j * LANES : (j + 1) * LANES] = slab_ref[pl.ds(start, rows, stride=fibres), :]


def join_kernel(fibres, *refs):
    *pieces, out_ref = refs
    count = len(pieces)
    rows, width = pieces[0].shape
    share = width // LANES
    for d, piece in enumerate(pieces):
        source = lax.rem(lax.axis_index("mode") - d + count, count)
        for j in range(share):
            start = source * share + j
            out_ref[pl.ds(start, rows, stride=fibres), :] = piece[:, j * LANES : (j + 1) * LANES]


def call(kernel, out_shapes, scratch, *operands, **options):
    whole = pl.BlockSpec(memory_space=pltpu.VMEM)
    return pl.pallas_call(
        kernel,
        out_shape=[jax.ShapeDtypeStruct(shape, jnp.float32) for shape in out_shapes],
        in_specs=[whole] * len(operands),
        out_specs=[whole] * len(out_shapes),
        scratch_shapes=[pltpu.VMEM(shape, jnp.float32) for shape in scratch],
        compiler_params=pltpu.CompilerParams(vmem_limit_bytes=VMEM_BYTES),
        **options,
    )(*operands)


def exchange(block, axis, bit):
    size = lax.axis_size(axis)
    return lax.ppermute(block, axis, [(k, k ^ bit) for k in range(size)])


def bits_of(axis):
    return [1 << b for b in range(lax.axis_size(axis).bit_length() - 1)]


def plane_exchange(block, stages, d):
    inner = lax.axis_size("rb")
    flip = 0
    for index, (axis, bit) in enumerate(stages[1:]):
        flip |= (d >> index & 1) * (bit if axis == "rb" else bit * inner)
    size = inner * lax.axis_size("ra")
    return lax.ppermute(block, ("ra", "rb"), [(k, k ^ flip) for k in range(size)])


def all_reduce(kept, sent, stages):
    members = 1 << (len(stages) - 1)
    share = kept.shape[0] // members
    far_first = range(members - 1, 0, -1)
    got = exchange(sent, *stages[0])

    def summed(d):
        place = slice(d * share, (d + 1) * share)
        return kept[place] + got[place]

    arrived = []
    for d in far_first:
        part = summed(d)
        arrived.append(plane_exchange(part, stages, d))
    held = summed(0)
    for part in arrived:
        held = held + part
    for bit in bits_of("mode"):
        held = held + exchange(held, "mode", bit)
    whole = {0: held}
    for d in far_first:
        whole[d] = plane_exchange(held, stages, d)
    held = jnp.concatenate([whole[d] for d in range(members)])
    return [held, exchange(held, *stages[0])]


def turned(blocks, count, here):
    return jnp.stack(
        [
            lax.dynamic_index_in_dim(blocks, (here - d) % count, 0, keepdims=False)
            for d in range(count)
        ]
    )


def shifted(piece, d, count):
    return lax.ppermute(piece, "mode", [(k, (k + d) % count) for k in range(count)]) if d else piece


def body(density_slab, start_basis):
    count = lax.axis_size("mode")
    here = lax.axis_index("mode")
    rows, nj, nk = density_slab.shape
    width, rank = start_basis.shape
    stages = [(axis, bit) for axis in ("rb", "ra") for bit in bits_of(axis)]

    share = nj // count
    slab = density_slab.reshape(rows * nj, nk)
    far_first = sorted(range(1, count), key=lambda d: abs(d - count // 2))
    blocks = [None] * count
    for distances in (far_first[:1], far_first[1:] + [0]):
        picked = call(
            functools.partial(pick_kernel, distances, count, nj),
            [(rows, share * nk)] * len(distances),
            [],
            slab,
        )
        for d, piece in zip(distances, picked):
            blocks[d] = shifted(piece, d, count)

    def turn(matrix):
        if rows % LANES == 0:
            return matrix
        split = matrix.reshape(-1, count, rows).transpose(1, 0, 2)
        return turned(split, count, here).transpose(1, 0, 2).reshape(-1, width)

    def total(partials):
        kept, sent = partials
        return all_reduce(turn(kept), turn(sent), stages)

    half = [(rank // 2, width)] * 2
    inner_shape = (rank, share * nk)
    tall = (rank, width)
    work = (rank, 2 * rank)
    applied = total(
        call(
            functools.partial(first_kernel, count, stages),
            half,
            [tall],
            start_basis,
            *blocks,
        ),
    )
    turned_in = [turn(part) for part in applied]
    again = total(
        call(
            functools.partial(second_kernel, count, len(applied), stages),
            half,
            [tall],
            *turned_in,
            *blocks,
        ),
    )
    (factor,) = call(functools.partial(inner_kernel, stages), [work], [tall], *applied)
    for top in range(0, rank, HALF):
        (factor,) = call(functools.partial(step_kernel, top), [work], [(SUB, LANES)], factor)
    outward = call(
        functools.partial(last_kernel, count, len(again), stages),
        [(rank // count, share * nk)] * count,
        [work, tall, inner_shape, (SUB, LANES)],
        factor,
        *[turn(part) for part in again],
        *blocks,
    )
    back = [shifted(piece, d, count) for d, piece in enumerate(outward)]
    (out,) = call(functools.partial(join_kernel, nj), [(rank // count * nj, nk)], [], *back)
    return out.reshape(rank // count, nj, nk)


def solution(mesh):
    in_specs = (P("mode", "ra", "rb"), P())
    out_specs = P("mode", "ra", "rb")

    return jax.shard_map(body, mesh=mesh, in_specs=in_specs, out_specs=out_specs, check_vma=False)
```

```python
import functools

import jax
import jax.numpy as jnp
from jax import lax
from jax.experimental import pallas as pl
from jax.experimental.pallas import tpu as pltpu
from jax.sharding import PartitionSpec as P


SUB, LANES = 8, 128
HALF = LANES // 2
VMEM_BYTES = 20 * 2**20
LIFT = 2.0**20


def mm(a, b, a_dim, b_dim):
    return lax.dot_general(
        a,
        b,
        (((a_dim,), (b_dim,)), ((), ())),
        precision=lax.Precision.HIGHEST,
        preferred_element_type=jnp.float32,
    )


def eliminate(groups, ones):
    sub = lax.broadcasted_iota(jnp.int32, (SUB, LANES), 0)
    done = []
    for p in range(len(groups)):
        first = p * SUB
        rows = [jnp.broadcast_to(groups[p][j : j + 1, :], (SUB, LANES)) for j in range(SUB)]
        across = [
            jnp.broadcast_to(groups[p][:, first + j : first + j + 1], (SUB, LANES)) * ones for j in range(SUB)
        ]
        block = [
            [jnp.broadcast_to(across[j][i : i + 1, :], (SUB, LANES)) if j >= i else None for j in range(SUB)]
            for i in range(SUB)
        ]
        lower = [[None] * SUB for _ in range(SUB)]
        inverse = []
        for i in range(SUB):
            inverse.append(1.0 / block[i][i])
            for j in range(i + 1, SUB):
                lower[j][i] = block[i][j] * inverse[i]
            for j in range(i + 1, SUB):
                for m in range(j, SUB):
                    block[j][m] = block[j][m] - lower[j][i] * block[i][m]
            for j in range(i + 1, SUB):
                rows[j] = rows[j] - lower[j][i] * rows[i]
        scaled = [rows[i] * inverse[i] for i in range(SUB)]
        for g in range(p + 1, len(groups)):
            tile = groups[g]
            columns = [
                jnp.broadcast_to(tile[:, first + j : first + j + 1], (SUB, LANES)) for j in range(SUB)
            ]
            for i in range(SUB):
                for j in range(i + 1, SUB):
                    columns[j] = columns[j] - columns[i] * lower[j][i]
            for i in range(SUB):
                tile = tile - columns[i] * scaled[i]
            groups[g] = tile
        out = rows[0] * lax.rsqrt(block[0][0])
        for i in range(1, SUB):
            out = jnp.where(sub == i, rows[i] * lax.rsqrt(block[i][i]), out)
        done.append(out)
    return done


def begin(inner, work):
    order = inner.shape[0]
    row = lax.broadcasted_iota(jnp.int32, (order, order), 0)
    col = lax.broadcasted_iota(jnp.int32, (order, order), 1)
    work[:, :order] = inner
    work[:, order:] = (row == col).astype(jnp.float32)


def step(work, top, ones):
    order = work.shape[0]
    low = top + HALF
    lane = lax.broadcasted_iota(jnp.int32, (SUB, LANES), 1)
    sub = lax.broadcasted_iota(jnp.int32, (SUB, LANES), 0)
    groups = []
    for g in range(HALF // SUB):
        tile = work[top + g * SUB : top + (g + 1) * SUB, top:low]
        unit = (lane == sub + (g * SUB + HALF)).astype(jnp.float32)
        groups.append(jnp.concatenate([tile, unit[:, HALF:]], axis=1))
    small = jnp.concatenate([tile[:, HALF:] for tile in eliminate(groups, ones)], axis=0)
    wide = mm(small, work[top:low, :], 1, 0)
    if low < order:
        work[low:, :] = work[low:, :] - mm(wide[:, low:order], wide, 0, 0)
    work[top:low, :] = wide


def lanes(d, rows):
    if rows % LANES:
        return pl.ds(d * rows, rows)
    return pl.ds(pl.multiple_of((lax.axis_index("mode") ^ d) * rows, rows), rows)


def stage_side(stage):
    axis, bit = stage
    return lax.rem(lax.axis_index(axis) // bit, 2)


def row_places(stages, height):
    members = 1 << (len(stages) - 1)
    share = height // (2 * members)
    mine = sum((stage_side(stage) << index) for index, stage in enumerate(stages[1:]))
    side = stage_side(stages[0])
    return [
        [pl.ds(pl.multiple_of((top * members + (mine ^ d)) * share, share), share) for d in range(members)]
        for top in (side, 1 - side)
    ]


def gather_rows(parts, stages, matrix):
    for part, places in zip(parts, row_places(stages, matrix.shape[0])):
        share = part.shape[0] // len(places)
        for d, place in enumerate(places):
            matrix[place, :] = part[d * share : (d + 1) * share, :]


def spread_out(inner, blocks, outs, stages, matrix):
    rows = blocks[0].shape[0]
    for d, block in enumerate(blocks):
        matrix[:, lanes(d, rows)] = mm(inner, block[...], 1, 1)
    for out, places in zip(outs, row_places(stages, matrix.shape[0])):
        share = out.shape[0] // len(places)
        for d, place in enumerate(places):
            out[d * share : (d + 1) * share, :] = matrix[place, :]


def basis_term(basis_ref, block, d):
    rows = block.shape[0]
    place = pl.ds(pl.multiple_of((lax.axis_index("mode") ^ d) * rows, rows), rows)
    return mm(basis_ref[place, :], block[...], 0, 0)


def early_kernel(basis_ref, *refs):
    *blocks, out_ref = refs
    inner = basis_term(basis_ref, blocks[0], 0)
    for d, block in enumerate(blocks[1:], 1):
        inner = inner + basis_term(basis_ref, block, d)
    out_ref[...] = inner


def first_kernel(count, stages, basis_ref, early_ref, *refs):
    blocks, outs, matrix = refs[:count], refs[count:-1], refs[-1]
    inner = early_ref[...] + basis_term(basis_ref, blocks[-1], count - 1)
    spread_out(inner, blocks, outs, stages, matrix)


def second_kernel(count, inputs, stages, *refs):
    parts, blocks = refs[:inputs], refs[inputs : inputs + count]
    outs, matrix = refs[inputs + count : -1], refs[-1]
    rows = blocks[0].shape[0]
    gather_rows(parts, stages, matrix)
    inner = None
    for d, block in enumerate(blocks):
        term = mm(matrix[:, lanes(d, rows)], block[...], 1, 0)
        inner = term if inner is None else inner + term
    spread_out(inner * LIFT, blocks, outs, stages, matrix)


def inner_kernel(stages, *refs):
    *parts, work, matrix = refs
    gather_rows(parts, stages, matrix)
    whole = matrix[...]
    begin(mm(whole, whole, 1, 1), work)


def step_kernel(top, work_ref, work, ones):
    ones[...] = jnp.ones_like(ones)
    work[...] = work_ref[...]
    step(work, top, ones[...])


def last_kernel(count, inputs, stages, work_ref, *refs):
    parts, blocks = refs[:inputs], refs[inputs : inputs + count]
    outs, (work, matrix, held, ones) = refs[inputs + count : -4], refs[-4:]
    rank, rows = matrix.shape[0], blocks[0].shape[0]
    gather_rows(parts, stages, matrix)
    factor = work_ref[:, rank:] * (1.0 / LIFT)
    inner = None
    projected = None
    for d, block in enumerate(blocks):
        basis = mm(factor, matrix[:, lanes(d, rows)], 1, 0)
        term = mm(basis, basis, 1, 1)
        inner = term if inner is None else inner + term
        term = mm(basis, block[...], 1, 0)
        projected = term if projected is None else projected + term
    held[...] = projected
    begin(inner, work)
    ones[...] = jnp.ones_like(ones)
    for top in range(0, rank, HALF):
        step(work, top, ones[...])
    held[...] = mm(work[:, rank:], held[...], 1, 0)
    here = lax.axis_index("mode")
    part = rank // count
    for d, out in enumerate(outs):
        place = pl.ds(pl.multiple_of((here ^ d) * part, part), part)
        out[...] = held[place, :]


def pick_kernel(distances, fibres, slab_ref, *outs):
    rows, width = outs[0].shape
    share = width // LANES
    for d, out in zip(distances, outs):
        target = lax.axis_index("mode") ^ d
        for j in range(share):
            start = target * share + j
            out[:, j * LANES : (j + 1) * LANES] = slab_ref[pl.ds(start, rows, stride=fibres), :]


def join_kernel(fibres, *refs):
    *pieces, out_ref = refs
    rows, width = pieces[0].shape
    share = width // LANES
    for d, piece in enumerate(pieces):
        source = lax.axis_index("mode") ^ d
        for j in range(share):
            start = source * share + j
            out_ref[pl.ds(start, rows, stride=fibres), :] = piece[:, j * LANES : (j + 1) * LANES]


def call(kernel, out_shapes, scratch, *operands, **options):
    whole = pl.BlockSpec(memory_space=pltpu.VMEM)
    return pl.pallas_call(
        kernel,
        out_shape=[jax.ShapeDtypeStruct(shape, jnp.float32) for shape in out_shapes],
        in_specs=[whole] * len(operands),
        out_specs=[whole] * len(out_shapes),
        scratch_shapes=[pltpu.VMEM(shape, jnp.float32) for shape in scratch],
        compiler_params=pltpu.CompilerParams(vmem_limit_bytes=VMEM_BYTES),
        **options,
    )(*operands)


def exchange(block, axis, bit):
    size = lax.axis_size(axis)
    return lax.ppermute(block, axis, [(k, k ^ bit) for k in range(size)])


def bits_of(axis):
    return [1 << b for b in range(lax.axis_size(axis).bit_length() - 1)]


def plane_exchange(block, stages, d):
    inner = lax.axis_size("rb")
    flip = 0
    for index, (axis, bit) in enumerate(stages[1:]):
        flip |= (d >> index & 1) * (bit if axis == "rb" else bit * inner)
    size = inner * lax.axis_size("ra")
    return lax.ppermute(block, ("ra", "rb"), [(k, k ^ flip) for k in range(size)])


def all_reduce(kept, sent, stages):
    members = 1 << (len(stages) - 1)
    share = kept.shape[0] // members
    far_first = range(members - 1, 0, -1)
    got = exchange(sent, *stages[0])

    def summed(d):
        place = slice(d * share, (d + 1) * share)
        return kept[place] + got[place]

    arrived = []
    for d in far_first:
        part = summed(d)
        arrived.append(plane_exchange(part, stages, d))
    held = summed(0)
    for part in arrived:
        held = held + part
    for bit in bits_of("mode"):
        held = held + exchange(held, "mode", bit)
    whole = {0: held}
    for d in far_first:
        whole[d] = plane_exchange(held, stages, d)
    held = jnp.concatenate([whole[d] for d in range(members)])
    return [held, exchange(held, *stages[0])]


def turned(blocks, count, here):
    return jnp.stack(
        [
            lax.dynamic_index_in_dim(blocks, here ^ d, 0, keepdims=False)
            for d in range(count)
        ]
    )


def body(density_slab, start_basis):
    count = lax.axis_size("mode")
    here = lax.axis_index("mode")
    rows, nj, nk = density_slab.shape
    width, rank = start_basis.shape
    stages = [(axis, bit) for axis in ("rb", "ra") for bit in bits_of(axis)]

    share = nj // count
    slab = density_slab.reshape(rows * nj, nk)
    far_first = sorted(range(1, count), key=lambda d: (d < count // 2, d))
    blocks = [None] * count
    for distances in (far_first[:1], far_first[1:] + [0]):
        picked = call(
            functools.partial(pick_kernel, distances, nj),
            [(rows, share * nk)] * len(distances),
            [],
            slab,
        )
        for d, piece in zip(distances, picked):
            blocks[d] = exchange(piece, "mode", d) if d else piece

    def turn(matrix):
        if rows % LANES == 0:
            return matrix
        split = matrix.reshape(-1, count, rows).transpose(1, 0, 2)
        return turned(split, count, here).transpose(1, 0, 2).reshape(-1, width)

    def total(partials):
        kept, sent = partials
        return all_reduce(turn(kept), turn(sent), stages)

    half = [(rank // 2, width)] * 2
    inner_shape = (rank, share * nk)
    tall = (rank, width)
    work = (rank, 2 * rank)
    (early,) = call(early_kernel, [inner_shape], [], start_basis, *blocks[:-1])
    applied = total(
        call(
            functools.partial(first_kernel, count, stages),
            half,
            [tall],
            start_basis,
            early,
            *blocks,
        ),
    )
    turned_in = [turn(part) for part in applied]
    again = total(
        call(
            functools.partial(second_kernel, count, len(applied), stages),
            half,
            [tall],
            *turned_in,
            *blocks,
        ),
    )
    (factor,) = call(functools.partial(inner_kernel, stages), [work], [tall], *applied)
    for top in range(0, rank, HALF):
        (factor,) = call(functools.partial(step_kernel, top), [work], [(SUB, LANES)], factor)
    outward = call(
        functools.partial(last_kernel, count, len(again), stages),
        [(rank // count, share * nk)] * count,
        [work, tall, inner_shape, (SUB, LANES)],
        factor,
        *[turn(part) for part in again],
        *blocks,
    )
    back = list(outward)
    for d in far_first:
        back[d] = exchange(outward[d], "mode", d)
    (out,) = call(functools.partial(join_kernel, nj), [(rank // count * nj, nk)], [], *back)
    return out.reshape(rank // count, nj, nk)


def solution(mesh):
    in_specs = (P("mode", "ra", "rb"), P())
    out_specs = P("mode", "ra", "rb")

    return jax.shard_map(body, mesh=mesh, in_specs=in_specs, out_specs=out_specs, check_vma=False)
```

```python
import functools

import jax
import jax.numpy as jnp
from jax import lax
from jax.experimental import pallas as pl
from jax.experimental.pallas import tpu as pltpu
from jax.sharding import PartitionSpec as P


SUB, LANES = 8, 128
PARTS = 8
HALF = LANES // 2
VMEM_BYTES = 20 * 2**20
LIFT = 2.0**20


def mm(a, b, a_dim, b_dim):
    return lax.dot_general(
        a,
        b,
        (((a_dim,), (b_dim,)), ((), ())),
        precision=lax.Precision.HIGHEST,
        preferred_element_type=jnp.float32,
    )


def eliminate(groups, ones):
    sub = lax.broadcasted_iota(jnp.int32, (SUB, LANES), 0)
    done = []
    for p in range(len(groups)):
        first = p * SUB
        rows = [jnp.broadcast_to(groups[p][j : j + 1, :], (SUB, LANES)) for j in range(SUB)]
        across = [
            jnp.broadcast_to(groups[p][:, first + j : first + j + 1], (SUB, LANES)) * ones for j in range(SUB)
        ]
        block = [
            [jnp.broadcast_to(across[j][i : i + 1, :], (SUB, LANES)) if j >= i else None for j in range(SUB)]
            for i in range(SUB)
        ]
        lower = [[None] * SUB for _ in range(SUB)]
        inverse = []
        for i in range(SUB):
            inverse.append(1.0 / block[i][i])
            for j in range(i + 1, SUB):
                lower[j][i] = block[i][j] * inverse[i]
            for j in range(i + 1, SUB):
                for m in range(j, SUB):
                    block[j][m] = block[j][m] - lower[j][i] * block[i][m]
            for j in range(i + 1, SUB):
                rows[j] = rows[j] - lower[j][i] * rows[i]
        scaled = [rows[i] * inverse[i] for i in range(SUB)]
        for g in range(p + 1, len(groups)):
            tile = groups[g]
            columns = [
                jnp.broadcast_to(tile[:, first + j : first + j + 1], (SUB, LANES)) for j in range(SUB)
            ]
            for i in range(SUB):
                for j in range(i + 1, SUB):
                    columns[j] = columns[j] - columns[i] * lower[j][i]
            for i in range(SUB):
                tile = tile - columns[i] * scaled[i]
            groups[g] = tile
        out = rows[0] * lax.rsqrt(block[0][0])
        for i in range(1, SUB):
            out = jnp.where(sub == i, rows[i] * lax.rsqrt(block[i][i]), out)
        done.append(out)
    return done


def begin(inner, work):
    order = inner.shape[0]
    row = lax.broadcasted_iota(jnp.int32, (order, order), 0)
    col = lax.broadcasted_iota(jnp.int32, (order, order), 1)
    work[:, :order] = inner
    work[:, order:] = (row == col).astype(jnp.float32)


def step(work, top, ones):
    order = work.shape[0]
    low = top + HALF
    lane = lax.broadcasted_iota(jnp.int32, (SUB, LANES), 1)
    sub = lax.broadcasted_iota(jnp.int32, (SUB, LANES), 0)
    groups = []
    for g in range(HALF // SUB):
        tile = work[top + g * SUB : top + (g + 1) * SUB, top:low]
        unit = (lane == sub + (g * SUB + HALF)).astype(jnp.float32)
        groups.append(jnp.concatenate([tile, unit[:, HALF:]], axis=1))
    small = jnp.concatenate([tile[:, HALF:] for tile in eliminate(groups, ones)], axis=0)
    wide = mm(small, work[top:low, :], 1, 0)
    if low < order:
        work[low:, :] = work[low:, :] - mm(wide[:, low:order], wide, 0, 0)
    work[top:low, :] = wide


def lanes(d, rows):
    if rows % LANES:
        return pl.ds(d * rows, rows)
    return pl.ds(pl.multiple_of((lax.axis_index("mode") ^ d) * rows, rows), rows)


def stage_side(stage):
    axis, bit = stage
    return lax.rem(lax.axis_index(axis) // bit, 2)


def row_places(stages, height):
    members = 1 << (len(stages) - 1)
    share = height // (2 * members)
    mine = sum((stage_side(stage) << index) for index, stage in enumerate(stages[1:]))
    side = stage_side(stages[0])
    return [
        [pl.ds(pl.multiple_of((top * members + (mine ^ d)) * share, share), share) for d in range(members)]
        for top in (side, 1 - side)
    ]


def gather_rows(parts, stages, matrix):
    for part, places in zip(parts, row_places(stages, matrix.shape[0])):
        share = part.shape[0] // len(places)
        for d, place in enumerate(places):
            matrix[place, :] = part[d * share : (d + 1) * share, :]


def spread_out(inner, blocks, outs, stages, matrix):
    rows = blocks[0].shape[0]
    for d, block in enumerate(blocks):
        matrix[:, lanes(d, rows)] = mm(inner, block[...], 1, 1)
    for out, places in zip(outs, row_places(stages, matrix.shape[0])):
        share = out.shape[0] // len(places)
        for d, place in enumerate(places):
            out[d * share : (d + 1) * share, :] = matrix[place, :]


def basis_term(basis_ref, block, d):
    rows = block.shape[0]
    place = pl.ds(pl.multiple_of((lax.axis_index("mode") ^ d) * rows, rows), rows)
    return mm(basis_ref[place, :], block[...], 0, 0)


def early_kernel(basis_ref, *refs):
    *blocks, out_ref = refs
    inner = basis_term(basis_ref, blocks[0], 0)
    for d, block in enumerate(blocks[1:], 1):
        inner = inner + basis_term(basis_ref, block, d)
    out_ref[...] = inner


def first_kernel(count, stages, basis_ref, early_ref, *refs):
    blocks, outs, matrix = refs[:count], refs[count:-1], refs[-1]
    inner = early_ref[...] + basis_term(basis_ref, blocks[-1], count - 1)
    spread_out(inner, blocks, outs, stages, matrix)


def second_kernel(count, inputs, arrived, stages, *refs):
    parts, blocks = refs[:inputs], refs[inputs : inputs + count]
    outs, matrix = refs[inputs + count : -1], refs[-1]
    rows = blocks[0].shape[0]
    gather_rows(parts, arrived, matrix)
    inner = None
    for d, block in enumerate(blocks):
        term = mm(matrix[:, lanes(d, rows)], block[...], 1, 0)
        inner = term if inner is None else inner + term
    spread_out(inner * LIFT, blocks, outs, stages, matrix)


def inner_kernel(stages, *refs):
    *parts, work, matrix = refs
    gather_rows(parts, stages, matrix)
    whole = matrix[...]
    begin(mm(whole, whole, 1, 1), work)


def step_kernel(top, work_ref, work, ones):
    ones[...] = jnp.ones_like(ones)
    work[...] = work_ref[...]
    step(work, top, ones[...])


def last_kernel(count, inputs, stages, work_ref, *refs):
    parts, blocks = refs[:inputs], refs[inputs : inputs + count]
    outs, (work, matrix, held, ones) = refs[inputs + count : -4], refs[-4:]
    rank, rows = matrix.shape[0], blocks[0].shape[0]
    gather_rows(parts, stages, matrix)
    factor = work_ref[:, rank:] * (1.0 / LIFT)
    inner = None
    projected = None
    for d, block in enumerate(blocks):
        basis = mm(factor, matrix[:, lanes(d, rows)], 1, 0)
        term = mm(basis, basis, 1, 1)
        inner = term if inner is None else inner + term
        term = mm(basis, block[...], 1, 0)
        projected = term if projected is None else projected + term
    held[...] = projected
    begin(inner, work)
    ones[...] = jnp.ones_like(ones)
    for top in range(0, rank, HALF):
        step(work, top, ones[...])
    held[...] = mm(work[:, rank:], held[...], 1, 0)
    here = lax.axis_index("mode")
    part = rank // count
    for d, out in enumerate(outs):
        place = pl.ds(pl.multiple_of((here ^ d) * part, part), part)
        out[...] = held[place, :]


def pick_kernel(distances, fibres, slab_ref, *refs):
    *outs, slab, sems = refs
    parts = sems.shape[0]
    height, rows = slab.shape[0] // parts, outs[0].shape[0] // parts
    share = outs[0].shape[1] // LANES
    copies = []
    for part in range(parts):
        place = pl.ds(part * height, height)
        copies.append(pltpu.make_async_copy(slab_ref.at[place, :], slab.at[place, :], sems.at[part]))
        copies[-1].start()
    for part, copy in enumerate(copies):
        copy.wait()
        for d, out in zip(distances, outs):
            target = lax.axis_index("mode") ^ d
            for j in range(share):
                start = part * height + target * share + j
                out[part * rows : (part + 1) * rows, j * LANES : (j + 1) * LANES] = slab[
                    pl.ds(start, rows, stride=fibres), :
                ]


def pick(distances, fibres, out_shape, slab):
    return pl.pallas_call(
        functools.partial(pick_kernel, distances, fibres),
        out_shape=[jax.ShapeDtypeStruct(out_shape, jnp.float32)] * len(distances),
        in_specs=[pl.BlockSpec(memory_space=pltpu.HBM)],
        out_specs=[pl.BlockSpec(memory_space=pltpu.VMEM)] * len(distances),
        scratch_shapes=[pltpu.VMEM(slab.shape, jnp.float32), pltpu.SemaphoreType.DMA((PARTS,))],
        compiler_params=pltpu.CompilerParams(vmem_limit_bytes=VMEM_BYTES),
    )(slab)


def join_kernel(fibres, *refs):
    *pieces, out_ref = refs
    rows, width = pieces[0].shape
    share = width // LANES
    for d, piece in enumerate(pieces):
        source = lax.axis_index("mode") ^ d
        for j in range(share):
            start = source * share + j
            out_ref[pl.ds(start, rows, stride=fibres), :] = piece[:, j * LANES : (j + 1) * LANES]


def call(kernel, out_shapes, scratch, *operands, **options):
    whole = pl.BlockSpec(memory_space=pltpu.VMEM)
    return pl.pallas_call(
        kernel,
        out_shape=[jax.ShapeDtypeStruct(shape, jnp.float32) for shape in out_shapes],
        in_specs=[whole] * len(operands),
        out_specs=[whole] * len(out_shapes),
        scratch_shapes=[pltpu.VMEM(shape, jnp.float32) for shape in scratch],
        compiler_params=pltpu.CompilerParams(vmem_limit_bytes=VMEM_BYTES),
        **options,
    )(*operands)


def exchange(block, axis, bit):
    size = lax.axis_size(axis)
    return lax.ppermute(block, axis, [(k, k ^ bit) for k in range(size)])


def bits_of(axis):
    return [1 << b for b in range(lax.axis_size(axis).bit_length() - 1)]


def plane_exchange(block, stages, d):
    axes = ("mode", "ra", "rb")
    sizes = [lax.axis_size(axis) for axis in axes]
    strides = {"mode": sizes[1] * sizes[2], "ra": sizes[2], "rb": 1}
    flip = 0
    for index, (axis, bit) in enumerate(stages[1:]):
        flip |= (d >> index & 1) * bit * strides[axis]
    return lax.ppermute(block, axes, [(k, k ^ flip) for k in range(sizes[0] * sizes[1] * sizes[2])])


def all_reduce(kept, sent, stages):
    members = 1 << (len(stages) - 1)
    share = kept.shape[0] // members
    far_first = range(members - 1, 0, -1)
    got = exchange(sent, *stages[0])

    def summed(d):
        place = slice(d * share, (d + 1) * share)
        return kept[place] + got[place]

    arrived = []
    for d in far_first:
        part = summed(d)
        arrived.append(plane_exchange(part, stages, d))
    held = summed(0)
    for part in arrived:
        held = held + part
    for bit in bits_of("mode"):
        if ("mode", bit) in stages:
            continue
        held = held + exchange(held, "mode", bit)
    whole = {0: held}
    for d in far_first:
        whole[d] = plane_exchange(held, stages, d)
    held = jnp.concatenate([whole[d] for d in range(members)])
    return [held, exchange(held, *stages[0])]


def turned(blocks, count, here):
    return jnp.stack(
        [
            lax.dynamic_index_in_dim(blocks, here ^ d, 0, keepdims=False)
            for d in range(count)
        ]
    )


def body(density_slab, start_basis):
    count = lax.axis_size("mode")
    here = lax.axis_index("mode")
    rows, nj, nk = density_slab.shape
    width, rank = start_basis.shape
    stages = [(axis, bit) for axis in ("rb", "ra") for bit in bits_of(axis)]
    wider = stages + [("mode", 1)]
    if rank >> len(wider) < SUB:
        wider = stages

    share = nj // count
    slab = pltpu.with_memory_space_constraint(density_slab.reshape(rows * nj, nk), pltpu.HBM)
    far_first = sorted(range(1, count), key=lambda d: (d < count // 2, d))
    blocks = [None] * count
    picked = []
    for distances in (far_first[:1], far_first[1:] + [0]):
        picked += pick(distances, nj, (rows, share * nk), slab)
    for d, piece in zip(far_first + [0], picked):
        blocks[d] = exchange(piece, "mode", d) if d else piece

    def turn(matrix):
        if rows % LANES == 0:
            return matrix
        split = matrix.reshape(-1, count, rows).transpose(1, 0, 2)
        return turned(split, count, here).transpose(1, 0, 2).reshape(-1, width)

    def total(partials, stages):
        kept, sent = partials
        return all_reduce(turn(kept), turn(sent), stages)

    half = [(rank // 2, width)] * 2
    inner_shape = (rank, share * nk)
    tall = (rank, width)
    work = (rank, 2 * rank)
    (early,) = call(early_kernel, [inner_shape], [], start_basis, *blocks[:-1])
    applied = total(
        call(
            functools.partial(first_kernel, count, wider),
            half,
            [tall],
            start_basis,
            early,
            *blocks,
        ),
        wider,
    )
    turned_in = [turn(part) for part in applied]
    again = total(
        call(
            functools.partial(second_kernel, count, len(applied), wider, stages),
            half,
            [tall],
            *turned_in,
            *blocks,
        ),
        stages,
    )
    (factor,) = call(functools.partial(inner_kernel, wider), [work], [tall], *applied)
    for top in range(0, rank, HALF):
        (factor,) = call(functools.partial(step_kernel, top), [work], [(SUB, LANES)], factor)
    outward = call(
        functools.partial(last_kernel, count, len(again), stages),
        [(rank // count, share * nk)] * count,
        [work, tall, inner_shape, (SUB, LANES)],
        factor,
        *[turn(part) for part in again],
        *blocks,
    )
    back = list(outward)
    for d in far_first:
        back[d] = exchange(outward[d], "mode", d)
    (out,) = call(functools.partial(join_kernel, nj), [(rank // count * nj, nk)], [], *back)
    return out.reshape(rank // count, nj, nk)


def solution(mesh):
    in_specs = (P("mode", "ra", "rb"), P())
    out_specs = P("mode", "ra", "rb")

    return jax.shard_map(body, mesh=mesh, in_specs=in_specs, out_specs=out_specs, check_vma=False)
```

```python
import functools

import jax
import jax.numpy as jnp
from jax import lax
from jax.experimental import pallas as pl
from jax.experimental.pallas import tpu as pltpu
from jax.sharding import PartitionSpec as P


SUB, LANES = 8, 128
PARTS = 8
HALF = LANES // 2
VMEM_BYTES = 20 * 2**20
LIFT = 2.0**20


def mm(a, b, a_dim, b_dim):
    return lax.dot_general(
        a,
        b,
        (((a_dim,), (b_dim,)), ((), ())),
        precision=lax.Precision.HIGHEST,
        preferred_element_type=jnp.float32,
    )


def eliminate(groups, ones):
    sub = lax.broadcasted_iota(jnp.int32, (SUB, LANES), 0)
    done = []
    for p in range(len(groups)):
        first = p * SUB
        rows = [jnp.broadcast_to(groups[p][j : j + 1, :], (SUB, LANES)) for j in range(SUB)]
        across = [
            jnp.broadcast_to(groups[p][:, first + j : first + j + 1], (SUB, LANES)) * ones for j in range(SUB)
        ]
        block = [
            [jnp.broadcast_to(across[j][i : i + 1, :], (SUB, LANES)) if j >= i else None for j in range(SUB)]
            for i in range(SUB)
        ]
        lower = [[None] * SUB for _ in range(SUB)]
        inverse = []
        for i in range(SUB):
            inverse.append(1.0 / block[i][i])
            for j in range(i + 1, SUB):
                lower[j][i] = block[i][j] * inverse[i]
            for j in range(i + 1, SUB):
                for m in range(j, SUB):
                    block[j][m] = block[j][m] - lower[j][i] * block[i][m]
            for j in range(i + 1, SUB):
                rows[j] = rows[j] - lower[j][i] * rows[i]
        scaled = [rows[i] * inverse[i] for i in range(SUB)]
        for g in range(p + 1, len(groups)):
            tile = groups[g]
            columns = [
                jnp.broadcast_to(tile[:, first + j : first + j + 1], (SUB, LANES)) for j in range(SUB)
            ]
            for i in range(SUB):
                for j in range(i + 1, SUB):
                    columns[j] = columns[j] - columns[i] * lower[j][i]
            for i in range(SUB):
                tile = tile - columns[i] * scaled[i]
            groups[g] = tile
        out = rows[0] * lax.rsqrt(block[0][0])
        for i in range(1, SUB):
            out = jnp.where(sub == i, rows[i] * lax.rsqrt(block[i][i]), out)
        done.append(out)
    return done


def begin(inner, work):
    order = inner.shape[0]
    row = lax.broadcasted_iota(jnp.int32, (order, order), 0)
    col = lax.broadcasted_iota(jnp.int32, (order, order), 1)
    work[:, :order] = inner
    work[:, order:] = (row == col).astype(jnp.float32)


def step(work, top, ones):
    order = work.shape[0]
    low = top + HALF
    lane = lax.broadcasted_iota(jnp.int32, (SUB, LANES), 1)
    sub = lax.broadcasted_iota(jnp.int32, (SUB, LANES), 0)
    groups = []
    for g in range(HALF // SUB):
        tile = work[top + g * SUB : top + (g + 1) * SUB, top:low]
        unit = (lane == sub + (g * SUB + HALF)).astype(jnp.float32)
        groups.append(jnp.concatenate([tile, unit[:, HALF:]], axis=1))
    small = jnp.concatenate([tile[:, HALF:] for tile in eliminate(groups, ones)], axis=0)
    wide = mm(small, work[top:low, :], 1, 0)
    if low < order:
        work[low:, :] = work[low:, :] - mm(wide[:, low:order], wide, 0, 0)
    work[top:low, :] = wide


def stage_side(stage):
    axis, bit = stage
    return lax.rem(lax.axis_index(axis) // bit, 2)


def lanes(e, half, rows):
    if rows % LANES:
        return pl.ds(e * rows, rows)
    here = lax.rem(lax.axis_index("mode"), half)
    return pl.ds(pl.multiple_of((here ^ e) * rows, rows), rows)


def half_of(blocks, first, kept):
    half = len(blocks) // 2
    top = (lax.axis_index("mode") // half) ^ stage_side(first)
    lower, upper = (0, half) if kept else (half, 0)
    return [jnp.where(top == 0, blocks[lower + e][...], blocks[upper + e][...]) for e in range(half)]


def row_places(stages, height):
    members = 1 << (len(stages) - 1)
    share = height // members
    mine = sum((stage_side(stage) << index) for index, stage in enumerate(stages[1:]))
    return [pl.ds(pl.multiple_of((mine ^ d) * share, share), share) for d in range(members)]


def absolute(part, stages, matrix):
    places = row_places(stages, matrix.shape[0])
    share = matrix.shape[0] // len(places)
    for d, place in enumerate(places):
        matrix[place, :] = part[d * share : (d + 1) * share, :]
    return matrix[...]


def spread(inner, blocks, first, kept, out):
    chosen = half_of(blocks, first, kept)
    for e, block in enumerate(chosen):
        out[:, lanes(e, len(chosen), block.shape[0])] = mm(inner, block, 1, 1)


def collect(part, blocks, first, kept):
    chosen = half_of(blocks, first, kept)
    inner = None
    for e, block in enumerate(chosen):
        term = mm(part[:, lanes(e, len(chosen), block.shape[0])], block, 1, 0)
        inner = term if inner is None else inner + term
    return inner


def basis_term(basis_ref, block, d):
    rows = block.shape[0]
    place = pl.ds(pl.multiple_of((lax.axis_index("mode") ^ d) * rows, rows), rows)
    return mm(basis_ref[place, :], block[...], 0, 0)


def early_kernel(basis_ref, *refs):
    *blocks, out_ref = refs
    inner = basis_term(basis_ref, blocks[0], 0)
    for d, block in enumerate(blocks[1:], 1):
        inner = inner + basis_term(basis_ref, block, d)
    out_ref[...] = inner


def first_kernel(stages, basis_ref, early_ref, *refs):
    *blocks, inner_ref, sent_ref, held = refs
    held[...] = early_ref[...] + basis_term(basis_ref, blocks[-1], len(blocks) - 1)
    share = held.shape[0] >> (len(stages) - 1)
    for d, place in enumerate(row_places(stages, held.shape[0])):
        inner_ref[d * share : (d + 1) * share, :] = held[place, :]
    spread(inner_ref[...], blocks, stages[0], False, sent_ref)


def keep_kernel(first, inner_ref, *refs):
    *blocks, kept_ref = refs
    spread(inner_ref[...], blocks, first, True, kept_ref)


def collect_kernel(first, part_ref, *refs):
    *blocks, out_ref = refs
    out_ref[...] = collect(part_ref, blocks, first, True)


def second_kernel(first, early_ref, part_ref, *refs):
    *blocks, inner_ref, sent_ref = refs
    inner_ref[...] = (early_ref[...] + collect(part_ref, blocks, first, False)) * LIFT
    spread(inner_ref[...], blocks, first, False, sent_ref)


def inner_kernel(stages, kept_ref, got_ref, work, matrix):
    inner = None
    for part in (kept_ref, got_ref):
        whole = absolute(part, stages, matrix)
        term = mm(whole, whole, 1, 1)
        inner = term if inner is None else inner + term
    begin(inner, work)


def step_kernel(top, work_ref, work, ones):
    ones[...] = jnp.ones_like(ones)
    work[...] = work_ref[...]
    step(work, top, ones[...])


def basis_half(work_ref, part, blocks, stages, kept, matrix):
    rank = matrix.shape[0]
    factor = work_ref[:, rank:] * (1.0 / LIFT)
    matrix[...] = mm(factor, absolute(part, stages, matrix), 1, 0)
    return mm(matrix[...], matrix[...], 1, 1), collect(matrix, blocks, stages[0], kept)


def half_kernel(stages, work_ref, part_ref, *refs):
    *blocks, inner_ref, projected_ref, matrix = refs
    inner_ref[...], projected_ref[...] = basis_half(work_ref, part_ref, blocks, stages, True, matrix)


def last_kernel(count, stages, work_ref, part_ref, inner_ref, projected_ref, *refs):
    blocks = refs[:count]
    outs, (work, matrix, held, ones) = refs[count:-4], refs[-4:]
    rank = matrix.shape[0]
    inner, projected = basis_half(work_ref, part_ref, blocks, stages, False, matrix)
    held[...] = projected_ref[...] + projected
    begin(inner_ref[...] + inner, work)
    ones[...] = jnp.ones_like(ones)
    for top in range(0, rank, HALF):
        step(work, top, ones[...])
    held[...] = mm(work[:, rank:], held[...], 1, 0)
    here = lax.axis_index("mode")
    part = rank // count
    for d, out in enumerate(outs):
        out[...] = held[pl.ds(pl.multiple_of((here ^ d) * part, part), part), :]


def pick_kernel(distances, fibres, slab_ref, *refs):
    *outs, slab, sems = refs
    parts = sems.shape[0]
    height, rows = slab.shape[0] // parts, outs[0].shape[0] // parts
    share = outs[0].shape[1] // LANES
    copies = []
    for part in range(parts):
        place = pl.ds(part * height, height)
        copies.append(pltpu.make_async_copy(slab_ref.at[place, :], slab.at[place, :], sems.at[part]))
        copies[-1].start()
    for part, copy in enumerate(copies):
        copy.wait()
        for d, out in zip(distances, outs):
            target = lax.axis_index("mode") ^ d
            for j in range(share):
                start = part * height + target * share + j
                out[part * rows : (part + 1) * rows, j * LANES : (j + 1) * LANES] = slab[
                    pl.ds(start, rows, stride=fibres), :
                ]


def pick(distances, fibres, out_shape, slab):
    return pl.pallas_call(
        functools.partial(pick_kernel, distances, fibres),
        out_shape=[jax.ShapeDtypeStruct(out_shape, jnp.float32)] * len(distances),
        in_specs=[pl.BlockSpec(memory_space=pltpu.HBM)],
        out_specs=[pl.BlockSpec(memory_space=pltpu.VMEM)] * len(distances),
        scratch_shapes=[pltpu.VMEM(slab.shape, jnp.float32), pltpu.SemaphoreType.DMA((PARTS,))],
        compiler_params=pltpu.CompilerParams(vmem_limit_bytes=VMEM_BYTES),
    )(slab)


def join_kernel(fibres, *refs):
    *pieces, out_ref = refs
    rows, width = pieces[0].shape
    share = width // LANES
    for d, piece in enumerate(pieces):
        source = lax.axis_index("mode") ^ d
        for j in range(share):
            start = source * share + j
            out_ref[pl.ds(start, rows, stride=fibres), :] = piece[:, j * LANES : (j + 1) * LANES]


def call(kernel, out_shapes, scratch, *operands, **options):
    whole = pl.BlockSpec(memory_space=pltpu.VMEM)
    return pl.pallas_call(
        kernel,
        out_shape=[jax.ShapeDtypeStruct(shape, jnp.float32) for shape in out_shapes],
        in_specs=[whole] * len(operands),
        out_specs=[whole] * len(out_shapes),
        scratch_shapes=[pltpu.VMEM(shape, jnp.float32) for shape in scratch],
        compiler_params=pltpu.CompilerParams(vmem_limit_bytes=VMEM_BYTES),
        **options,
    )(*operands)


def exchange(block, axis, bit):
    size = lax.axis_size(axis)
    return lax.ppermute(block, axis, [(k, k ^ bit) for k in range(size)])


def bits_of(axis):
    return [1 << b for b in range(lax.axis_size(axis).bit_length() - 1)]


def plane_exchange(block, stages, d):
    axes = ("mode", "ra", "rb")
    sizes = [lax.axis_size(axis) for axis in axes]
    strides = {"mode": sizes[1] * sizes[2], "ra": sizes[2], "rb": 1}
    flip = 0
    for index, (axis, bit) in enumerate(stages[1:]):
        flip |= (d >> index & 1) * bit * strides[axis]
    return lax.ppermute(block, axes, [(k, k ^ flip) for k in range(sizes[0] * sizes[1] * sizes[2])])


def all_reduce(sent, keep, stages):
    members = 1 << (len(stages) - 1)
    share = sent.shape[0] // members
    far_first = range(members - 1, 0, -1)
    got = exchange(sent, *stages[0])
    kept = keep()

    def summed(d):
        place = slice(d * share, (d + 1) * share)
        return kept[place] + got[place]

    arrived = []
    for d in far_first:
        part = summed(d)
        arrived.append(plane_exchange(part, stages, d))
    held = summed(0)
    for part in arrived:
        held = held + part
    for bit in bits_of("mode"):
        if ("mode", bit) in stages:
            continue
        held = held + exchange(held, "mode", bit)
    whole = {0: held}
    for d in far_first:
        whole[d] = plane_exchange(held, stages, d)
    held = jnp.concatenate([whole[d] for d in range(members)])
    return [held, exchange(held, *stages[0])]


def turned(blocks, count, here):
    return jnp.stack(
        [
            lax.dynamic_index_in_dim(blocks, here ^ d, 0, keepdims=False)
            for d in range(count)
        ]
    )


def body(density_slab, start_basis):
    count = lax.axis_size("mode")
    here = lax.axis_index("mode")
    rows, nj, nk = density_slab.shape
    _, rank = start_basis.shape
    stages = [(axis, bit) for axis in ("rb", "ra") for bit in bits_of(axis)]

    share = nj // count
    slab = pltpu.with_memory_space_constraint(density_slab.reshape(rows * nj, nk), pltpu.HBM)
    far_first = sorted(range(1, count), key=lambda d: (d < count // 2, d))
    blocks = [None] * count
    picked = []
    for distances in (far_first[:1], far_first[1:] + [0]):
        picked += pick(distances, nj, (rows, share * nk), slab)
    for d, piece in zip(far_first + [0], picked):
        blocks[d] = exchange(piece, "mode", d) if d else piece

    half = count // 2
    first = stages[0]

    def turn(matrix):
        if rows % LANES == 0:
            return matrix
        split = matrix.reshape(rank, half, rows).transpose(1, 0, 2)
        return turned(split, half, here % half).transpose(1, 0, 2).reshape(rank, half * rows)

    def total(inner, sent):
        def keep():
            (kept,) = call(functools.partial(keep_kernel, first), [column_half], [], inner, *blocks)
            return turn(kept)

        return all_reduce(turn(sent), keep, stages)

    inner_shape = (rank, share * nk)
    column_half = (rank, half * rows)
    work = (rank, 2 * rank)
    (early,) = call(early_kernel, [inner_shape], [], start_basis, *blocks[:-1])
    inner, sent = call(
        functools.partial(first_kernel, stages),
        [inner_shape, column_half],
        [inner_shape],
        start_basis,
        early,
        *blocks,
    )
    kept, got = total(inner, sent)
    (early,) = call(functools.partial(collect_kernel, first), [inner_shape], [], turn(kept), *blocks)
    inner, sent = call(
        functools.partial(second_kernel, first), [inner_shape, column_half], [], early, turn(got), *blocks
    )
    again, other = total(inner, sent)
    (factor,) = call(functools.partial(inner_kernel, stages), [work], [column_half], kept, got)
    for top in range(0, rank, HALF):
        (factor,) = call(functools.partial(step_kernel, top), [work], [(SUB, LANES)], factor)
    early = call(
        functools.partial(half_kernel, stages),
        [(rank, rank), inner_shape],
        [column_half],
        factor,
        turn(again),
        *blocks,
    )
    outward = call(
        functools.partial(last_kernel, count, stages),
        [(rank // count, share * nk)] * count,
        [work, column_half, inner_shape, (SUB, LANES)],
        factor,
        turn(other),
        *early,
        *blocks,
    )
    back = list(outward)
    for d in far_first:
        back[d] = exchange(outward[d], "mode", d)
    (out,) = call(functools.partial(join_kernel, nj), [(rank // count * nj, nk)], [], *back)
    return out.reshape(rank // count, nj, nk)


def solution(mesh):
    in_specs = (P("mode", "ra", "rb"), P())
    out_specs = P("mode", "ra", "rb")

    return jax.shard_map(body, mesh=mesh, in_specs=in_specs, out_specs=out_specs, check_vma=False)
```

```python
import functools

import jax
import jax.numpy as jnp
from jax import lax
from jax.experimental import pallas as pl
from jax.experimental.pallas import tpu as pltpu
from jax.sharding import PartitionSpec as P


SUB, LANES = 8, 128
PARTS = 8
HALF = LANES // 2
VMEM_BYTES = 20 * 2**20
LIFT = 2.0**20


def mm(a, b, a_dim, b_dim):
    return lax.dot_general(
        a,
        b,
        (((a_dim,), (b_dim,)), ((), ())),
        precision=lax.Precision.HIGHEST,
        preferred_element_type=jnp.float32,
    )


def eliminate(groups, ones):
    sub = lax.broadcasted_iota(jnp.int32, (SUB, LANES), 0)
    done = []
    for p in range(len(groups)):
        first = p * SUB
        rows = [jnp.broadcast_to(groups[p][j : j + 1, :], (SUB, LANES)) for j in range(SUB)]
        across = [
            jnp.broadcast_to(groups[p][:, first + j : first + j + 1], (SUB, LANES)) * ones for j in range(SUB)
        ]
        block = [
            [jnp.broadcast_to(across[j][i : i + 1, :], (SUB, LANES)) if j >= i else None for j in range(SUB)]
            for i in range(SUB)
        ]
        lower = [[None] * SUB for _ in range(SUB)]
        inverse = []
        for i in range(SUB):
            inverse.append(1.0 / block[i][i])
            for j in range(i + 1, SUB):
                lower[j][i] = block[i][j] * inverse[i]
            for j in range(i + 1, SUB):
                for m in range(j, SUB):
                    block[j][m] = block[j][m] - lower[j][i] * block[i][m]
            for j in range(i + 1, SUB):
                rows[j] = rows[j] - lower[j][i] * rows[i]
        scaled = [rows[i] * inverse[i] for i in range(SUB)]
        for g in range(p + 1, len(groups)):
            tile = groups[g]
            columns = [
                jnp.broadcast_to(tile[:, first + j : first + j + 1], (SUB, LANES)) for j in range(SUB)
            ]
            for i in range(SUB):
                for j in range(i + 1, SUB):
                    columns[j] = columns[j] - columns[i] * lower[j][i]
            for i in range(SUB):
                tile = tile - columns[i] * scaled[i]
            groups[g] = tile
        out = rows[0] * lax.rsqrt(block[0][0])
        for i in range(1, SUB):
            out = jnp.where(sub == i, rows[i] * lax.rsqrt(block[i][i]), out)
        done.append(out)
    return done


def begin(inner, work):
    order = inner.shape[0]
    row = lax.broadcasted_iota(jnp.int32, (order, order), 0)
    col = lax.broadcasted_iota(jnp.int32, (order, order), 1)
    work[:, :order] = inner
    work[:, order:] = (row == col).astype(jnp.float32)


def step(work, top, ones):
    order = work.shape[0]
    low = top + HALF
    lane = lax.broadcasted_iota(jnp.int32, (SUB, LANES), 1)
    sub = lax.broadcasted_iota(jnp.int32, (SUB, LANES), 0)
    groups = []
    for g in range(HALF // SUB):
        tile = work[top + g * SUB : top + (g + 1) * SUB, top:low]
        unit = (lane == sub + (g * SUB + HALF)).astype(jnp.float32)
        groups.append(jnp.concatenate([tile, unit[:, HALF:]], axis=1))
    small = jnp.concatenate([tile[:, HALF:] for tile in eliminate(groups, ones)], axis=0)
    left, right = low // LANES * LANES, -(-(order + low) // LANES) * LANES
    wide = mm(small, work[top:low, left:right], 1, 0)
    if low < order:
        update = mm(wide[:, low - left : order - left], wide, 0, 0)
        work[low:, left:right] = work[low:, left:right] - update
    work[top:low, left:right] = wide


def stage_side(stage):
    axis, bit = stage
    return lax.rem(lax.axis_index(axis) // bit, 2)


def lanes(e, half, rows):
    if rows % LANES:
        return pl.ds(e * rows, rows)
    here = lax.rem(lax.axis_index("mode"), half)
    return pl.ds(pl.multiple_of((here ^ e) * rows, rows), rows)


def half_of(blocks, first, kept):
    half = len(blocks) // 2
    top = (lax.axis_index("mode") // half) ^ stage_side(first)
    lower, upper = (0, half) if kept else (half, 0)
    return [jnp.where(top == 0, blocks[lower + e][...], blocks[upper + e][...]) for e in range(half)]


def row_places(stages, height):
    members = 1 << (len(stages) - 1)
    share = height // members
    mine = sum((stage_side(stage) << index) for index, stage in enumerate(stages[1:]))
    return [pl.ds(pl.multiple_of((mine ^ d) * share, share), share) for d in range(members)]


def absolute(part, stages, matrix):
    places = row_places(stages, matrix.shape[0])
    share = matrix.shape[0] // len(places)
    for d, place in enumerate(places):
        matrix[place, :] = part[d * share : (d + 1) * share, :]
    return matrix[...]


def spread(inner, blocks, first, kept, out):
    chosen = half_of(blocks, first, kept)
    for e, block in enumerate(chosen):
        out[:, lanes(e, len(chosen), block.shape[0])] = mm(inner, block, 1, 1)


def collect(part, blocks, first, kept):
    chosen = half_of(blocks, first, kept)
    inner = None
    for e, block in enumerate(chosen):
        term = mm(part[:, lanes(e, len(chosen), block.shape[0])], block, 1, 0)
        inner = term if inner is None else inner + term
    return inner


def basis_term(basis_ref, block, d):
    rows = block.shape[0]
    place = pl.ds(pl.multiple_of((lax.axis_index("mode") ^ d) * rows, rows), rows)
    return mm(basis_ref[place, :], block[...], 0, 0)


def early_kernel(basis_ref, *refs):
    *blocks, out_ref = refs
    inner = basis_term(basis_ref, blocks[0], 0)
    for d, block in enumerate(blocks[1:], 1):
        inner = inner + basis_term(basis_ref, block, d)
    out_ref[...] = inner


def first_kernel(stages, basis_ref, early_ref, *refs):
    *blocks, inner_ref, sent_ref, held = refs
    held[...] = early_ref[...] + basis_term(basis_ref, blocks[-1], len(blocks) - 1)
    share = held.shape[0] >> (len(stages) - 1)
    for d, place in enumerate(row_places(stages, held.shape[0])):
        inner_ref[d * share : (d + 1) * share, :] = held[place, :]
    spread(inner_ref[...], blocks, stages[0], False, sent_ref)


def keep_kernel(first, inner_ref, *refs):
    *blocks, kept_ref = refs
    spread(inner_ref[...], blocks, first, True, kept_ref)


def collect_kernel(first, part_ref, *refs):
    *blocks, out_ref = refs
    out_ref[...] = collect(part_ref, blocks, first, True)


def second_kernel(first, early_ref, part_ref, *refs):
    *blocks, inner_ref, sent_ref = refs
    inner_ref[...] = (early_ref[...] + collect(part_ref, blocks, first, False)) * LIFT
    spread(inner_ref[...], blocks, first, False, sent_ref)


def inner_kernel(stages, kept_ref, got_ref, work, matrix):
    inner = None
    for part in (kept_ref, got_ref):
        whole = absolute(part, stages, matrix)
        term = mm(whole, whole, 1, 1)
        inner = term if inner is None else inner + term
    begin(inner, work)


def step_kernel(top, work_ref, work, ones):
    ones[...] = jnp.ones_like(ones)
    work[...] = work_ref[...]
    step(work, top, ones[...])


def basis_half(work_ref, part, blocks, stages, kept, matrix):
    rank = matrix.shape[0]
    factor = work_ref[:, rank:] * (1.0 / LIFT)
    matrix[...] = mm(factor, absolute(part, stages, matrix), 1, 0)
    return mm(matrix[...], matrix[...], 1, 1), collect(matrix, blocks, stages[0], kept)


def half_kernel(stages, work_ref, part_ref, *refs):
    *blocks, inner_ref, projected_ref, matrix = refs
    inner_ref[...], projected_ref[...] = basis_half(work_ref, part_ref, blocks, stages, True, matrix)


def last_kernel(count, stages, work_ref, part_ref, inner_ref, projected_ref, *refs):
    blocks = refs[:count]
    outs, (work, matrix, held, ones) = refs[count:-4], refs[-4:]
    rank = matrix.shape[0]
    inner, projected = basis_half(work_ref, part_ref, blocks, stages, False, matrix)
    held[...] = projected_ref[...] + projected
    begin(inner_ref[...] + inner, work)
    ones[...] = jnp.ones_like(ones)
    for top in range(0, rank, HALF):
        step(work, top, ones[...])
    held[...] = mm(work[:, rank:], held[...], 1, 0)
    here = lax.axis_index("mode")
    part = rank // count
    for d, out in enumerate(outs):
        out[...] = held[pl.ds(pl.multiple_of((here ^ d) * part, part), part), :]


def pick_kernel(distances, fibres, slab_ref, *refs):
    *outs, slab, sems = refs
    parts = sems.shape[0]
    height, rows = slab.shape[0] // parts, outs[0].shape[0] // parts
    share = outs[0].shape[1] // LANES
    copies = []
    for part in range(parts):
        place = pl.ds(part * height, height)
        copies.append(pltpu.make_async_copy(slab_ref.at[place, :], slab.at[place, :], sems.at[part]))
        copies[-1].start()
    for part, copy in enumerate(copies):
        copy.wait()
        for d, out in zip(distances, outs):
            target = lax.axis_index("mode") ^ d
            for j in range(share):
                start = part * height + target * share + j
                out[part * rows : (part + 1) * rows, j * LANES : (j + 1) * LANES] = slab[
                    pl.ds(start, rows, stride=fibres), :
                ]


def pick(distances, fibres, out_shape, slab):
    return pl.pallas_call(
        functools.partial(pick_kernel, distances, fibres),
        out_shape=[jax.ShapeDtypeStruct(out_shape, jnp.float32)] * len(distances),
        in_specs=[pl.BlockSpec(memory_space=pltpu.HBM)],
        out_specs=[pl.BlockSpec(memory_space=pltpu.VMEM)] * len(distances),
        scratch_shapes=[pltpu.VMEM(slab.shape, jnp.float32), pltpu.SemaphoreType.DMA((PARTS,))],
        compiler_params=pltpu.CompilerParams(vmem_limit_bytes=VMEM_BYTES),
    )(slab)


def join_kernel(fibres, *refs):
    *pieces, out_ref = refs
    rows, width = pieces[0].shape
    share = width // LANES
    for d, piece in enumerate(pieces):
        source = lax.axis_index("mode") ^ d
        for j in range(share):
            start = source * share + j
            out_ref[pl.ds(start, rows, stride=fibres), :] = piece[:, j * LANES : (j + 1) * LANES]


def call(kernel, out_shapes, scratch, *operands, **options):
    whole = pl.BlockSpec(memory_space=pltpu.VMEM)
    return pl.pallas_call(
        kernel,
        out_shape=[jax.ShapeDtypeStruct(shape, jnp.float32) for shape in out_shapes],
        in_specs=[whole] * len(operands),
        out_specs=[whole] * len(out_shapes),
        scratch_shapes=[pltpu.VMEM(shape, jnp.float32) for shape in scratch],
        compiler_params=pltpu.CompilerParams(vmem_limit_bytes=VMEM_BYTES),
        **options,
    )(*operands)


def exchange(block, axis, bit):
    size = lax.axis_size(axis)
    return lax.ppermute(block, axis, [(k, k ^ bit) for k in range(size)])


def bits_of(axis):
    return [1 << b for b in range(lax.axis_size(axis).bit_length() - 1)]


def plane_exchange(block, stages, d):
    axes = ("mode", "ra", "rb")
    sizes = [lax.axis_size(axis) for axis in axes]
    strides = {"mode": sizes[1] * sizes[2], "ra": sizes[2], "rb": 1}
    flip = 0
    for index, (axis, bit) in enumerate(stages[1:]):
        flip |= (d >> index & 1) * bit * strides[axis]
    return lax.ppermute(block, axes, [(k, k ^ flip) for k in range(sizes[0] * sizes[1] * sizes[2])])


def all_reduce(sent, keep, stages):
    members = 1 << (len(stages) - 1)
    share = sent.shape[0] // members
    far_first = range(members - 1, 0, -1)
    got = exchange(sent, *stages[0])
    kept = keep()

    def summed(d):
        place = slice(d * share, (d + 1) * share)
        return kept[place] + got[place]

    arrived = []
    for d in far_first:
        part = summed(d)
        arrived.append(plane_exchange(part, stages, d))
    held = summed(0)
    for part in arrived:
        held = held + part
    for bit in bits_of("mode"):
        if ("mode", bit) in stages:
            continue
        held = held + exchange(held, "mode", bit)
    whole = {0: held}
    for d in far_first:
        whole[d] = plane_exchange(held, stages, d)
    held = jnp.concatenate([whole[d] for d in range(members)])
    return [held, exchange(held, *stages[0])]


def turned(blocks, count, here):
    return jnp.stack(
        [
            lax.dynamic_index_in_dim(blocks, here ^ d, 0, keepdims=False)
            for d in range(count)
        ]
    )


def body(density_slab, start_basis):
    count = lax.axis_size("mode")
    here = lax.axis_index("mode")
    rows, nj, nk = density_slab.shape
    _, rank = start_basis.shape
    stages = [(axis, bit) for axis in ("rb", "ra") for bit in bits_of(axis)]

    share = nj // count
    slab = pltpu.with_memory_space_constraint(density_slab.reshape(rows * nj, nk), pltpu.HBM)
    far_first = sorted(range(1, count), key=lambda d: (d < count // 2, d))
    blocks = [None] * count
    picked = []
    for distances in (far_first[:1], far_first[1:] + [0]):
        picked += pick(distances, nj, (rows, share * nk), slab)
    for d, piece in zip(far_first + [0], picked):
        blocks[d] = exchange(piece, "mode", d) if d else piece

    half = count // 2
    first = stages[0]

    def turn(matrix):
        if rows % LANES == 0:
            return matrix
        split = matrix.reshape(rank, half, rows).transpose(1, 0, 2)
        return turned(split, half, here % half).transpose(1, 0, 2).reshape(rank, half * rows)

    def total(inner, sent):
        def keep():
            (kept,) = call(functools.partial(keep_kernel, first), [column_half], [], inner, *blocks)
            return turn(kept)

        return all_reduce(turn(sent), keep, stages)

    inner_shape = (rank, share * nk)
    column_half = (rank, half * rows)
    work = (rank, 2 * rank)
    (early,) = call(early_kernel, [inner_shape], [], start_basis, *blocks[:-1])
    inner, sent = call(
        functools.partial(first_kernel, stages),
        [inner_shape, column_half],
        [inner_shape],
        start_basis,
        early,
        *blocks,
    )
    kept, got = total(inner, sent)
    (early,) = call(functools.partial(collect_kernel, first), [inner_shape], [], turn(kept), *blocks)
    inner, sent = call(
        functools.partial(second_kernel, first), [inner_shape, column_half], [], early, turn(got), *blocks
    )
    again, other = total(inner, sent)
    (factor,) = call(functools.partial(inner_kernel, stages), [work], [column_half], kept, got)
    for top in range(0, rank, HALF):
        (factor,) = call(functools.partial(step_kernel, top), [work], [(SUB, LANES)], factor)
    early = call(
        functools.partial(half_kernel, stages),
        [(rank, rank), inner_shape],
        [column_half],
        factor,
        turn(again),
        *blocks,
    )
    outward = call(
        functools.partial(last_kernel, count, stages),
        [(rank // count, share * nk)] * count,
        [work, column_half, inner_shape, (SUB, LANES)],
        factor,
        turn(other),
        *early,
        *blocks,
    )
    back = list(outward)
    for d in far_first:
        back[d] = exchange(outward[d], "mode", d)
    (out,) = call(functools.partial(join_kernel, nj), [(rank // count * nj, nk)], [], *back)
    return out.reshape(rank // count, nj, nk)


def solution(mesh):
    in_specs = (P("mode", "ra", "rb"), P())
    out_specs = P("mode", "ra", "rb")

    return jax.shard_map(body, mesh=mesh, in_specs=in_specs, out_specs=out_specs, check_vma=False)
```

```python
import functools

import jax
import jax.numpy as jnp
from jax import lax
from jax.experimental import pallas as pl
from jax.experimental.pallas import tpu as pltpu
from jax.sharding import PartitionSpec as P


SUB, LANES = 8, 128
PARTS = 8
HALF = LANES // 2
VMEM_BYTES = 20 * 2**20
LIFT = 2.0**20


def mm(a, b, a_dim, b_dim):
    return lax.dot_general(
        a,
        b,
        (((a_dim,), (b_dim,)), ((), ())),
        precision=lax.Precision.HIGHEST,
        preferred_element_type=jnp.float32,
    )


def eliminate(groups, ones):
    sub = lax.broadcasted_iota(jnp.int32, (SUB, LANES), 0)

    def columns_of(tile, first):
        return [jnp.broadcast_to(tile[:, first + j : first + j + 1], (SUB, LANES)) * ones for j in range(SUB)]

    def row_of(tile, j):
        return jnp.broadcast_to(tile[j : j + 1, :], (SUB, LANES))

    done = []
    across = columns_of(groups[0], 0)
    for p in range(len(groups)):
        first = p * SUB
        rows = [row_of(groups[p], j) for j in range(SUB)]
        upcoming = columns_of(groups[p + 1], first + SUB) if p + 1 < len(groups) else None
        block = [
            [row_of(across[j], i) if j >= i else None for j in range(SUB)] for i in range(SUB)
        ]
        lower = [[None] * SUB for _ in range(SUB)]
        inverse = []
        for i in range(SUB):
            inverse.append(1.0 / block[i][i])
            for j in range(i + 1, SUB):
                lower[j][i] = block[i][j] * inverse[i]
            for j in range(i + 1, SUB):
                for m in range(j, SUB):
                    block[j][m] = block[j][m] - lower[j][i] * block[i][m]
            for j in range(i + 1, SUB):
                rows[j] = rows[j] - lower[j][i] * rows[i]
        scaled = [rows[i] * inverse[i] for i in range(SUB)]
        for g in range(p + 1, len(groups)):
            tile = groups[g]
            columns = columns_of(tile, first)
            for i in range(SUB):
                for j in range(i + 1, SUB):
                    columns[j] = columns[j] - columns[i] * lower[j][i]
            if g == p + 1:
                for i in range(SUB):
                    weighted = columns[i] * inverse[i]
                    for j in range(SUB):
                        upcoming[j] = upcoming[j] - weighted * row_of(columns[i], j)
            for i in range(SUB):
                tile = tile - columns[i] * scaled[i]
            groups[g] = tile
        across = upcoming
        out = rows[0] * lax.rsqrt(block[0][0])
        for i in range(1, SUB):
            out = jnp.where(sub == i, rows[i] * lax.rsqrt(block[i][i]), out)
        done.append(out)
    return done


def begin(inner, work):
    order = inner.shape[0]
    row = lax.broadcasted_iota(jnp.int32, (order, order), 0)
    col = lax.broadcasted_iota(jnp.int32, (order, order), 1)
    work[:, :order] = inner
    work[:, order:] = (row == col).astype(jnp.float32)


def step(work, top, ones):
    order = work.shape[0]
    low = top + HALF
    lane = lax.broadcasted_iota(jnp.int32, (SUB, LANES), 1)
    sub = lax.broadcasted_iota(jnp.int32, (SUB, LANES), 0)
    groups = []
    for g in range(HALF // SUB):
        tile = work[top + g * SUB : top + (g + 1) * SUB, top:low]
        unit = (lane == sub + (g * SUB + HALF)).astype(jnp.float32)
        groups.append(jnp.concatenate([tile, unit[:, HALF:]], axis=1))
    small = jnp.concatenate([tile[:, HALF:] for tile in eliminate(groups, ones)], axis=0)
    left, right = low // LANES * LANES, -(-(order + low) // LANES) * LANES
    wide = mm(small, work[top:low, left:right], 1, 0)
    if low < order:
        update = mm(wide[:, low - left : order - left], wide, 0, 0)
        work[low:, left:right] = work[low:, left:right] - update
    work[top:low, left:right] = wide


def stage_side(stage):
    axis, bit = stage
    return lax.rem(lax.axis_index(axis) // bit, 2)


def lanes(e, half, rows):
    if rows % LANES:
        return pl.ds(e * rows, rows)
    here = lax.rem(lax.axis_index("mode"), half)
    return pl.ds(pl.multiple_of((here ^ e) * rows, rows), rows)


def half_of(blocks, first, kept):
    half = len(blocks) // 2
    top = (lax.axis_index("mode") // half) ^ stage_side(first)
    lower, upper = (0, half) if kept else (half, 0)
    return [jnp.where(top == 0, blocks[lower + e][...], blocks[upper + e][...]) for e in range(half)]


def row_places(stages, height):
    members = 1 << (len(stages) - 1)
    share = height // members
    mine = sum((stage_side(stage) << index) for index, stage in enumerate(stages[1:]))
    return [pl.ds(pl.multiple_of((mine ^ d) * share, share), share) for d in range(members)]


def absolute(part, stages, matrix):
    places = row_places(stages, matrix.shape[0])
    share = matrix.shape[0] // len(places)
    for d, place in enumerate(places):
        matrix[place, :] = part[d * share : (d + 1) * share, :]
    return matrix[...]


def spread(inner, blocks, first, kept, out):
    chosen = half_of(blocks, first, kept)
    for e, block in enumerate(chosen):
        out[:, lanes(e, len(chosen), block.shape[0])] = mm(inner, block, 1, 1)


def collect(part, blocks, first, kept):
    chosen = half_of(blocks, first, kept)
    inner = None
    for e, block in enumerate(chosen):
        term = mm(part[:, lanes(e, len(chosen), block.shape[0])], block, 1, 0)
        inner = term if inner is None else inner + term
    return inner


def basis_term(basis_ref, block, d):
    rows = block.shape[0]
    place = pl.ds(pl.multiple_of((lax.axis_index("mode") ^ d) * rows, rows), rows)
    return mm(basis_ref[place, :], block[...], 0, 0)


def early_kernel(basis_ref, *refs):
    *blocks, out_ref = refs
    inner = basis_term(basis_ref, blocks[0], 0)
    for d, block in enumerate(blocks[1:], 1):
        inner = inner + basis_term(basis_ref, block, d)
    out_ref[...] = inner


def first_kernel(stages, basis_ref, early_ref, *refs):
    *blocks, inner_ref, sent_ref, held = refs
    held[...] = early_ref[...] + basis_term(basis_ref, blocks[-1], len(blocks) - 1)
    share = held.shape[0] >> (len(stages) - 1)
    for d, place in enumerate(row_places(stages, held.shape[0])):
        inner_ref[d * share : (d + 1) * share, :] = held[place, :]
    spread(inner_ref[...], blocks, stages[0], False, sent_ref)


def keep_kernel(first, inner_ref, *refs):
    *blocks, kept_ref = refs
    spread(inner_ref[...], blocks, first, True, kept_ref)


def collect_kernel(first, part_ref, *refs):
    *blocks, out_ref = refs
    out_ref[...] = collect(part_ref, blocks, first, True)


def second_kernel(first, early_ref, part_ref, *refs):
    *blocks, inner_ref, sent_ref = refs
    inner_ref[...] = (early_ref[...] + collect(part_ref, blocks, first, False)) * LIFT
    spread(inner_ref[...], blocks, first, False, sent_ref)


def inner_kernel(stages, kept_ref, got_ref, work, matrix):
    inner = None
    for part in (kept_ref, got_ref):
        whole = absolute(part, stages, matrix)
        term = mm(whole, whole, 1, 1)
        inner = term if inner is None else inner + term
    begin(inner, work)


def step_kernel(top, work_ref, work, ones):
    ones[...] = jnp.ones_like(ones)
    work[...] = work_ref[...]
    step(work, top, ones[...])


def basis_half(work_ref, part, blocks, stages, kept, matrix):
    rank = matrix.shape[0]
    factor = work_ref[:, rank:] * (1.0 / LIFT)
    matrix[...] = mm(factor, absolute(part, stages, matrix), 1, 0)
    return mm(matrix[...], matrix[...], 1, 1), collect(matrix, blocks, stages[0], kept)


def half_kernel(stages, work_ref, part_ref, *refs):
    *blocks, inner_ref, projected_ref, matrix = refs
    inner_ref[...], projected_ref[...] = basis_half(work_ref, part_ref, blocks, stages, True, matrix)


def last_kernel(count, stages, work_ref, part_ref, inner_ref, projected_ref, *refs):
    blocks = refs[:count]
    outs, (work, matrix, held, ones) = refs[count:-4], refs[-4:]
    rank = matrix.shape[0]
    inner, projected = basis_half(work_ref, part_ref, blocks, stages, False, matrix)
    held[...] = projected_ref[...] + projected
    begin(inner_ref[...] + inner, work)
    ones[...] = jnp.ones_like(ones)
    for top in range(0, rank, HALF):
        step(work, top, ones[...])
    held[...] = mm(work[:, rank:], held[...], 1, 0)
    here = lax.axis_index("mode")
    part = rank // count
    for d, out in enumerate(outs):
        out[...] = held[pl.ds(pl.multiple_of((here ^ d) * part, part), part), :]


def pick_kernel(distances, fibres, slab_ref, *refs):
    *outs, slab, sems = refs
    parts = sems.shape[0]
    height, rows = slab.shape[0] // parts, outs[0].shape[0] // parts
    share = outs[0].shape[1] // LANES
    copies = []
    for part in range(parts):
        place = pl.ds(part * height, height)
        copies.append(pltpu.make_async_copy(slab_ref.at[place, :], slab.at[place, :], sems.at[part]))
        copies[-1].start()
    for part, copy in enumerate(copies):
        copy.wait()
        for d, out in zip(distances, outs):
            target = lax.axis_index("mode") ^ d
            for j in range(share):
                start = part * height + target * share + j
                out[part * rows : (part + 1) * rows, j * LANES : (j + 1) * LANES] = slab[
                    pl.ds(start, rows, stride=fibres), :
                ]


def pick(distances, fibres, out_shape, slab):
    return pl.pallas_call(
        functools.partial(pick_kernel, distances, fibres),
        out_shape=[jax.ShapeDtypeStruct(out_shape, jnp.float32)] * len(distances),
        in_specs=[pl.BlockSpec(memory_space=pltpu.HBM)],
        out_specs=[pl.BlockSpec(memory_space=pltpu.VMEM)] * len(distances),
        scratch_shapes=[pltpu.VMEM(slab.shape, jnp.float32), pltpu.SemaphoreType.DMA((PARTS,))],
        compiler_params=pltpu.CompilerParams(vmem_limit_bytes=VMEM_BYTES),
    )(slab)


def join_kernel(fibres, *refs):
    *pieces, out_ref = refs
    rows, width = pieces[0].shape
    share = width // LANES
    for d, piece in enumerate(pieces):
        source = lax.axis_index("mode") ^ d
        for j in range(share):
            start = source * share + j
            out_ref[pl.ds(start, rows, stride=fibres), :] = piece[:, j * LANES : (j + 1) * LANES]


def call(kernel, out_shapes, scratch, *operands, **options):
    whole = pl.BlockSpec(memory_space=pltpu.VMEM)
    return pl.pallas_call(
        kernel,
        out_shape=[jax.ShapeDtypeStruct(shape, jnp.float32) for shape in out_shapes],
        in_specs=[whole] * len(operands),
        out_specs=[whole] * len(out_shapes),
        scratch_shapes=[pltpu.VMEM(shape, jnp.float32) for shape in scratch],
        compiler_params=pltpu.CompilerParams(vmem_limit_bytes=VMEM_BYTES),
        **options,
    )(*operands)


def exchange(block, axis, bit):
    size = lax.axis_size(axis)
    return lax.ppermute(block, axis, [(k, k ^ bit) for k in range(size)])


def bits_of(axis):
    return [1 << b for b in range(lax.axis_size(axis).bit_length() - 1)]


def plane_exchange(block, stages, d):
    axes = ("mode", "ra", "rb")
    sizes = [lax.axis_size(axis) for axis in axes]
    strides = {"mode": sizes[1] * sizes[2], "ra": sizes[2], "rb": 1}
    flip = 0
    for index, (axis, bit) in enumerate(stages[1:]):
        flip |= (d >> index & 1) * bit * strides[axis]
    return lax.ppermute(block, axes, [(k, k ^ flip) for k in range(sizes[0] * sizes[1] * sizes[2])])


def all_reduce(sent, keep, stages):
    members = 1 << (len(stages) - 1)
    share = sent.shape[0] // members
    far_first = range(members - 1, 0, -1)
    got = exchange(sent, *stages[0])
    kept = keep()

    def summed(d):
        place = slice(d * share, (d + 1) * share)
        return kept[place] + got[place]

    arrived = []
    for d in far_first:
        part = summed(d)
        arrived.append(plane_exchange(part, stages, d))
    held = summed(0)
    for part in arrived:
        held = held + part
    for bit in bits_of("mode"):
        if ("mode", bit) in stages:
            continue
        held = held + exchange(held, "mode", bit)
    whole = {0: held}
    for d in far_first:
        whole[d] = plane_exchange(held, stages, d)
    held = jnp.concatenate([whole[d] for d in range(members)])
    return [held, exchange(held, *stages[0])]


def turned(blocks, count, here):
    return jnp.stack(
        [
            lax.dynamic_index_in_dim(blocks, here ^ d, 0, keepdims=False)
            for d in range(count)
        ]
    )


def body(density_slab, start_basis):
    count = lax.axis_size("mode")
    here = lax.axis_index("mode")
    rows, nj, nk = density_slab.shape
    _, rank = start_basis.shape
    stages = [(axis, bit) for axis in ("rb", "ra") for bit in bits_of(axis)]

    share = nj // count
    slab = pltpu.with_memory_space_constraint(density_slab.reshape(rows * nj, nk), pltpu.HBM)
    far_first = sorted(range(1, count), key=lambda d: (d < count // 2, d))
    blocks = [None] * count
    picked = []
    for distances in (far_first[:1], far_first[1:] + [0]):
        picked += pick(distances, nj, (rows, share * nk), slab)
    for d, piece in zip(far_first + [0], picked):
        blocks[d] = exchange(piece, "mode", d) if d else piece

    half = count // 2
    first = stages[0]

    def turn(matrix):
        if rows % LANES == 0:
            return matrix
        split = matrix.reshape(rank, half, rows).transpose(1, 0, 2)
        return turned(split, half, here % half).transpose(1, 0, 2).reshape(rank, half * rows)

    def total(inner, sent):
        def keep():
            (kept,) = call(functools.partial(keep_kernel, first), [column_half], [], inner, *blocks)
            return turn(kept)

        return all_reduce(turn(sent), keep, stages)

    inner_shape = (rank, share * nk)
    column_half = (rank, half * rows)
    work = (rank, 2 * rank)
    (early,) = call(early_kernel, [inner_shape], [], start_basis, *blocks[:-1])
    inner, sent = call(
        functools.partial(first_kernel, stages),
        [inner_shape, column_half],
        [inner_shape],
        start_basis,
        early,
        *blocks,
    )
    kept, got = total(inner, sent)
    (early,) = call(functools.partial(collect_kernel, first), [inner_shape], [], turn(kept), *blocks)
    inner, sent = call(
        functools.partial(second_kernel, first), [inner_shape, column_half], [], early, turn(got), *blocks
    )
    again, other = total(inner, sent)
    (factor,) = call(functools.partial(inner_kernel, stages), [work], [column_half], kept, got)
    for top in range(0, rank, HALF):
        (factor,) = call(functools.partial(step_kernel, top), [work], [(SUB, LANES)], factor)
    early = call(
        functools.partial(half_kernel, stages),
        [(rank, rank), inner_shape],
        [column_half],
        factor,
        turn(again),
        *blocks,
    )
    outward = call(
        functools.partial(last_kernel, count, stages),
        [(rank // count, share * nk)] * count,
        [work, column_half, inner_shape, (SUB, LANES)],
        factor,
        turn(other),
        *early,
        *blocks,
    )
    back = list(outward)
    for d in far_first:
        back[d] = exchange(outward[d], "mode", d)
    (out,) = call(functools.partial(join_kernel, nj), [(rank // count * nj, nk)], [], *back)
    return out.reshape(rank // count, nj, nk)


def solution(mesh):
    in_specs = (P("mode", "ra", "rb"), P())
    out_specs = P("mode", "ra", "rb")

    return jax.shard_map(body, mesh=mesh, in_specs=in_specs, out_specs=out_specs, check_vma=False)
```

```python
import functools

import jax
import jax.numpy as jnp
from jax import lax
from jax.experimental import pallas as pl
from jax.experimental.pallas import tpu as pltpu
from jax.sharding import PartitionSpec as P


SUB, LANES = 8, 128
PARTS = 4
HALF = LANES // 2
VMEM_BYTES = 20 * 2**20
LIFT = 2.0**20


def mm(a, b, a_dim, b_dim):
    return lax.dot_general(
        a,
        b,
        (((a_dim,), (b_dim,)), ((), ())),
        precision=lax.Precision.HIGHEST,
        preferred_element_type=jnp.float32,
    )


def eliminate(groups, ones):
    sub = lax.broadcasted_iota(jnp.int32, (SUB, LANES), 0)

    def columns_of(tile, first):
        return [jnp.broadcast_to(tile[:, first + j : first + j + 1], (SUB, LANES)) for j in range(SUB)]

    def row_of(tile, j):
        return jnp.broadcast_to(tile[j : j + 1, :], (SUB, LANES))

    done = []
    across = [column * ones for column in columns_of(groups[0], 0)]
    for p in range(len(groups)):
        first = p * SUB
        rows = [row_of(groups[p], j) for j in range(SUB)]
        upcoming = columns_of(groups[p + 1], first + SUB) if p + 1 < len(groups) else None
        block = [
            [row_of(across[j], i) if j >= i else None for j in range(SUB)] for i in range(SUB)
        ]
        lower = [[None] * SUB for _ in range(SUB)]
        inverse = []
        for i in range(SUB):
            inverse.append(1.0 / block[i][i])
            for j in range(i + 1, SUB):
                lower[j][i] = block[i][j] * inverse[i]
            for j in range(i + 1, SUB):
                for m in range(j, SUB):
                    block[j][m] = block[j][m] - lower[j][i] * block[i][m]
            for j in range(i + 1, SUB):
                rows[j] = rows[j] - lower[j][i] * rows[i]
        scaled = [rows[i] * inverse[i] for i in range(SUB)]
        for g in range(p + 1, len(groups)):
            tile = groups[g]
            columns = columns_of(tile, first)
            if g == p + 1:
                columns[0] = columns[0] * ones
            for i in range(SUB):
                for j in range(i + 1, SUB):
                    columns[j] = columns[j] - columns[i] * lower[j][i]
            if g == p + 1:
                for i in range(SUB):
                    weighted = columns[i] * inverse[i]
                    for j in range(SUB):
                        upcoming[j] = upcoming[j] - weighted * row_of(columns[i], j)
            for i in range(SUB):
                tile = tile - columns[i] * scaled[i]
            groups[g] = tile
        across = upcoming
        out = rows[0] * lax.rsqrt(block[0][0])
        for i in range(1, SUB):
            out = jnp.where(sub == i, rows[i] * lax.rsqrt(block[i][i]), out)
        done.append(out)
    return done


def begin(inner, work):
    order = inner.shape[0]
    row = lax.broadcasted_iota(jnp.int32, (order, order), 0)
    col = lax.broadcasted_iota(jnp.int32, (order, order), 1)
    work[:, :order] = inner
    work[:, order:] = (row == col).astype(jnp.float32)


def step(work, top, ones):
    order = work.shape[0]
    low = top + HALF
    lane = lax.broadcasted_iota(jnp.int32, (SUB, LANES), 1)
    sub = lax.broadcasted_iota(jnp.int32, (SUB, LANES), 0)
    groups = []
    for g in range(HALF // SUB):
        tile = work[top + g * SUB : top + (g + 1) * SUB, top:low]
        unit = (lane == sub + (g * SUB + HALF)).astype(jnp.float32)
        groups.append(jnp.concatenate([tile, unit[:, HALF:]], axis=1))
    small = jnp.concatenate([tile[:, HALF:] for tile in eliminate(groups, ones)], axis=0)
    left, right = low // LANES * LANES, -(-(order + low) // LANES) * LANES
    wide = mm(small, work[top:low, left:right], 1, 0)
    if low < order:
        update = mm(wide[:, low - left : order - left], wide, 0, 0)
        work[low:, left:right] = work[low:, left:right] - update
    work[top:low, left:right] = wide


def stage_side(stage):
    axis, bit = stage
    return lax.rem(lax.axis_index(axis) // bit, 2)


def lanes(e, half, rows):
    if rows % LANES:
        return pl.ds(e * rows, rows)
    here = lax.rem(lax.axis_index("mode"), half)
    return pl.ds(pl.multiple_of((here ^ e) * rows, rows), rows)


def half_of(blocks, first, kept):
    half = len(blocks) // 2
    top = (lax.axis_index("mode") // half) ^ stage_side(first)
    lower, upper = (0, half) if kept else (half, 0)
    return [jnp.where(top == 0, blocks[lower + e][...], blocks[upper + e][...]) for e in range(half)]


def row_places(stages, height):
    members = 1 << (len(stages) - 1)
    share = height // members
    mine = sum((stage_side(stage) << index) for index, stage in enumerate(stages[1:]))
    return [pl.ds(pl.multiple_of((mine ^ d) * share, share), share) for d in range(members)]


def absolute(part, stages, matrix):
    places = row_places(stages, matrix.shape[0])
    share = matrix.shape[0] // len(places)
    for d, place in enumerate(places):
        matrix[place, :] = part[d * share : (d + 1) * share, :]
    return matrix[...]


def spread(inner, blocks, first, kept, out):
    chosen = half_of(blocks, first, kept)
    for e, block in enumerate(chosen):
        out[:, lanes(e, len(chosen), block.shape[0])] = mm(inner, block, 1, 1)


def collect(part, blocks, first, kept):
    chosen = half_of(blocks, first, kept)
    inner = None
    for e, block in enumerate(chosen):
        term = mm(part[:, lanes(e, len(chosen), block.shape[0])], block, 1, 0)
        inner = term if inner is None else inner + term
    return inner


def basis_term(basis_ref, block, d):
    rows = block.shape[0]
    place = pl.ds(pl.multiple_of((lax.axis_index("mode") ^ d) * rows, rows), rows)
    return mm(basis_ref[place, :], block[...], 0, 0)


def early_kernel(basis_ref, *refs):
    *blocks, out_ref = refs
    inner = basis_term(basis_ref, blocks[0], 0)
    for d, block in enumerate(blocks[1:], 1):
        inner = inner + basis_term(basis_ref, block, d)
    out_ref[...] = inner


def first_kernel(stages, basis_ref, early_ref, *refs):
    *blocks, inner_ref, sent_ref, held = refs
    held[...] = early_ref[...] + basis_term(basis_ref, blocks[-1], len(blocks) - 1)
    share = held.shape[0] >> (len(stages) - 1)
    for d, place in enumerate(row_places(stages, held.shape[0])):
        inner_ref[d * share : (d + 1) * share, :] = held[place, :]
    spread(inner_ref[...], blocks, stages[0], False, sent_ref)


def keep_kernel(first, inner_ref, *refs):
    *blocks, kept_ref = refs
    spread(inner_ref[...], blocks, first, True, kept_ref)


def collect_kernel(first, part_ref, *refs):
    *blocks, out_ref = refs
    out_ref[...] = collect(part_ref, blocks, first, True)


def second_kernel(first, early_ref, part_ref, *refs):
    *blocks, inner_ref, sent_ref = refs
    inner_ref[...] = (early_ref[...] + collect(part_ref, blocks, first, False)) * LIFT
    spread(inner_ref[...], blocks, first, False, sent_ref)


def inner_kernel(stages, kept_ref, got_ref, work, matrix):
    inner = None
    for part in (kept_ref, got_ref):
        whole = absolute(part, stages, matrix)
        term = mm(whole, whole, 1, 1)
        inner = term if inner is None else inner + term
    begin(inner, work)


def step_kernel(top, work_ref, work, ones):
    ones[...] = jnp.ones_like(ones)
    work[...] = work_ref[...]
    step(work, top, ones[...])


def basis_half(work_ref, part, blocks, stages, kept, matrix):
    rank = matrix.shape[0]
    factor = work_ref[:, rank:] * (1.0 / LIFT)
    matrix[...] = mm(factor, absolute(part, stages, matrix), 1, 0)
    return mm(matrix[...], matrix[...], 1, 1), collect(matrix, blocks, stages[0], kept)


def half_kernel(stages, work_ref, part_ref, *refs):
    *blocks, inner_ref, projected_ref, matrix = refs
    inner_ref[...], projected_ref[...] = basis_half(work_ref, part_ref, blocks, stages, True, matrix)


def last_kernel(count, stages, work_ref, part_ref, inner_ref, projected_ref, *refs):
    blocks = refs[:count]
    outs, (work, matrix, held, ones) = refs[count:-4], refs[-4:]
    rank = matrix.shape[0]
    inner, projected = basis_half(work_ref, part_ref, blocks, stages, False, matrix)
    held[...] = projected_ref[...] + projected
    begin(inner_ref[...] + inner, work)
    ones[...] = jnp.ones_like(ones)
    for top in range(0, rank, HALF):
        step(work, top, ones[...])
    held[...] = mm(work[:, rank:], held[...], 1, 0)
    here = lax.axis_index("mode")
    part = rank // count
    for d, out in enumerate(outs):
        out[...] = held[pl.ds(pl.multiple_of((here ^ d) * part, part), part), :]


def pick_kernel(distances, fibres, slab_ref, *refs):
    *outs, slab, sems = refs
    parts = sems.shape[0]
    height, rows = slab.shape[0] // parts, outs[0].shape[0] // parts
    share = outs[0].shape[1] // LANES
    copies = []
    for part in range(parts):
        place = pl.ds(part * height, height)
        copies.append(pltpu.make_async_copy(slab_ref.at[place, :], slab.at[place, :], sems.at[part]))
        copies[-1].start()
    for part, copy in enumerate(copies):
        copy.wait()
        for d, out in zip(distances, outs):
            target = lax.axis_index("mode") ^ d
            for j in range(share):
                start = part * height + target * share + j
                out[part * rows : (part + 1) * rows, j * LANES : (j + 1) * LANES] = slab[
                    pl.ds(start, rows, stride=fibres), :
                ]


def pick(distances, fibres, out_shape, slab):
    return pl.pallas_call(
        functools.partial(pick_kernel, distances, fibres),
        out_shape=[jax.ShapeDtypeStruct(out_shape, jnp.float32)] * len(distances),
        in_specs=[pl.BlockSpec(memory_space=pltpu.HBM)],
        out_specs=[pl.BlockSpec(memory_space=pltpu.VMEM)] * len(distances),
        scratch_shapes=[pltpu.VMEM(slab.shape, jnp.float32), pltpu.SemaphoreType.DMA((PARTS,))],
        compiler_params=pltpu.CompilerParams(vmem_limit_bytes=VMEM_BYTES),
    )(slab)


def join_kernel(fibres, *refs):
    *pieces, out_ref = refs
    rows, width = pieces[0].shape
    share = width // LANES
    for d, piece in enumerate(pieces):
        source = lax.axis_index("mode") ^ d
        for j in range(share):
            start = source * share + j
            out_ref[pl.ds(start, rows, stride=fibres), :] = piece[:, j * LANES : (j + 1) * LANES]


def call(kernel, out_shapes, scratch, *operands, **options):
    whole = pl.BlockSpec(memory_space=pltpu.VMEM)
    return pl.pallas_call(
        kernel,
        out_shape=[jax.ShapeDtypeStruct(shape, jnp.float32) for shape in out_shapes],
        in_specs=[whole] * len(operands),
        out_specs=[whole] * len(out_shapes),
        scratch_shapes=[pltpu.VMEM(shape, jnp.float32) for shape in scratch],
        compiler_params=pltpu.CompilerParams(vmem_limit_bytes=VMEM_BYTES),
        **options,
    )(*operands)


def exchange(block, axis, bit):
    size = lax.axis_size(axis)
    return lax.ppermute(block, axis, [(k, k ^ bit) for k in range(size)])


def bits_of(axis):
    return [1 << b for b in range(lax.axis_size(axis).bit_length() - 1)]


def plane_exchange(block, stages, d):
    axes = ("mode", "ra", "rb")
    sizes = [lax.axis_size(axis) for axis in axes]
    strides = {"mode": sizes[1] * sizes[2], "ra": sizes[2], "rb": 1}
    flip = 0
    for index, (axis, bit) in enumerate(stages[1:]):
        flip |= (d >> index & 1) * bit * strides[axis]
    return lax.ppermute(block, axes, [(k, k ^ flip) for k in range(sizes[0] * sizes[1] * sizes[2])])


def all_reduce(sent, keep, stages):
    members = 1 << (len(stages) - 1)
    share = sent.shape[0] // members
    far_first = range(members - 1, 0, -1)
    got = exchange(sent, *stages[0])
    kept = keep()

    def summed(d):
        place = slice(d * share, (d + 1) * share)
        return kept[place] + got[place]

    arrived = []
    for d in far_first:
        part = summed(d)
        arrived.append(plane_exchange(part, stages, d))
    held = summed(0)
    for part in arrived:
        held = held + part
    for bit in bits_of("mode"):
        if ("mode", bit) in stages:
            continue
        held = held + exchange(held, "mode", bit)
    whole = {0: held}
    for d in far_first:
        whole[d] = plane_exchange(held, stages, d)
    held = jnp.concatenate([whole[d] for d in range(members)])
    return [held, exchange(held, *stages[0])]


def turned(blocks, count, here):
    return jnp.stack(
        [
            lax.dynamic_index_in_dim(blocks, here ^ d, 0, keepdims=False)
            for d in range(count)
        ]
    )


def body(density_slab, start_basis):
    count = lax.axis_size("mode")
    here = lax.axis_index("mode")
    rows, nj, nk = density_slab.shape
    _, rank = start_basis.shape
    stages = [(axis, bit) for axis in ("rb", "ra") for bit in bits_of(axis)]

    share = nj // count
    slab = pltpu.with_memory_space_constraint(density_slab.reshape(rows * nj, nk), pltpu.HBM)
    far_first = sorted(range(1, count), key=lambda d: (d < count // 2, d))
    blocks = [None] * count
    picked = []
    for distances in (far_first[:1], far_first[1:] + [0]):
        picked += pick(distances, nj, (rows, share * nk), slab)
    for d, piece in zip(far_first + [0], picked):
        blocks[d] = exchange(piece, "mode", d) if d else piece

    half = count // 2
    first = stages[0]

    def turn(matrix):
        if rows % LANES == 0:
            return matrix
        split = matrix.reshape(rank, half, rows).transpose(1, 0, 2)
        return turned(split, half, here % half).transpose(1, 0, 2).reshape(rank, half * rows)

    def total(inner, sent):
        def keep():
            (kept,) = call(functools.partial(keep_kernel, first), [column_half], [], inner, *blocks)
            return turn(kept)

        return all_reduce(turn(sent), keep, stages)

    inner_shape = (rank, share * nk)
    column_half = (rank, half * rows)
    work = (rank, 2 * rank)
    (early,) = call(early_kernel, [inner_shape], [], start_basis, *blocks[:-1])
    inner, sent = call(
        functools.partial(first_kernel, stages),
        [inner_shape, column_half],
        [inner_shape],
        start_basis,
        early,
        *blocks,
    )
    kept, got = total(inner, sent)
    (early,) = call(functools.partial(collect_kernel, first), [inner_shape], [], turn(kept), *blocks)
    inner, sent = call(
        functools.partial(second_kernel, first), [inner_shape, column_half], [], early, turn(got), *blocks
    )
    again, other = total(inner, sent)
    (factor,) = call(functools.partial(inner_kernel, stages), [work], [column_half], kept, got)
    for top in range(0, rank, HALF):
        (factor,) = call(functools.partial(step_kernel, top), [work], [(SUB, LANES)], factor)
    early = call(
        functools.partial(half_kernel, stages),
        [(rank, rank), inner_shape],
        [column_half],
        factor,
        turn(again),
        *blocks,
    )
    outward = call(
        functools.partial(last_kernel, count, stages),
        [(rank // count, share * nk)] * count,
        [work, column_half, inner_shape, (SUB, LANES)],
        factor,
        turn(other),
        *early,
        *blocks,
    )
    back = list(outward)
    for d in far_first:
        back[d] = exchange(outward[d], "mode", d)
    (out,) = call(functools.partial(join_kernel, nj), [(rank // count * nj, nk)], [], *back)
    return out.reshape(rank // count, nj, nk)


def solution(mesh):
    in_specs = (P("mode", "ra", "rb"), P())
    out_specs = P("mode", "ra", "rb")

    return jax.shard_map(body, mesh=mesh, in_specs=in_specs, out_specs=out_specs, check_vma=False)
```
